32 devices in a mesh: col: 4 (over y, x), row: 8 (over z, core).
Axes of the slice: x: 2, y: 2, z: 4, core: 2. Of those that a mesh axis runs over, the one named last changes fastest.
Arguments:
- covariance: float32 [12288, 12288], P('row', 'col'), may hold values from -2 to 2, as said below
- wfs_map: int32 [12288], P('row'), may hold values from 0 to 5
- noise_var: float32 [6], replicated, may hold values from 0.5 to 2
- targets: float32 [12288, 2048], P('row', 'col'), may hold values from -0.6 to 0.6
- target_pos: float32 [2, 2048], replicated, may hold values from -1 to 1
- layer_strength: float32 [35], replicated, may hold values from 0.005 to 0.05
- layer_scale: float32 [35], replicated, may hold values from 0.2 to 2
- tile_layer: int32 [16], replicated, may hold values from 0 to 34
Outputs:
- updated: float32 [12288, 12288], P('row', 'col')
- panel_factor: float32 [12288, 256], P('row')
- reconstructor: float32 [12288, 2048], P('row', 'col')
- error_cov: float32 [2048, 2048], P('row', 'col')
The draws below stay inside these ranges and needn't reach their ends.
Inputs may be any that keep to these rules, and one draw needn't show every extreme that they name: `covariance`: symmetric and positive semidefinite; its diagonal lies between 0.5 and 2.
All inputs are finite; a program needn't handle non-finite values.
Results may differ from the reference program's by a relative error of at most 0.0003.
Values sent between devices are 32-bit elements; how exact they have to be, the bound alone decides.
A program may use at most 128 MiB of HBM per device.

```python
import math
import jax
import jax.numpy as jnp
from jax import lax

M = 12288
PB = 256
TC = 2048
TILE = 128
NL = 35
NWFS = 6


def draw_covariance(key, part):
    key_base = jax.random.fold_in(key, 11)
    indices = jnp.arange(M, dtype=jnp.int32)
    base_draw = jax.random.normal(key_base, (M, PB), jnp.float32)
    row_scale = jnp.ones((M,), jnp.float32)
    smooth = base_draw
    weight = 1.0
    for lag in range(1, 8):
        weight = weight * 0.8
        smooth = smooth + weight * jnp.roll(base_draw, lag, axis=0)
    gram = jnp.dot(smooth, smooth.T, precision=lax.Precision.HIGHEST)
    norms = jnp.sum(smooth * smooth, axis=1)
    inverse = row_scale / jnp.sqrt(norms)
    gram = gram * inverse[:, None] * inverse[None, :]
    symmetric = jnp.where(indices[:, None] >= indices[None, :], gram, gram.T)
    symmetric = jnp.clip(symmetric, -2.0, 2.0)
    return symmetric.at[indices, indices].set(row_scale)


def place_ends(entries, stream_key, smallest, high):
    extent = entries.shape
    spot = [jax.random.randint(jax.random.fold_in(stream_key, axis), (), 0, extent[axis]) for axis in range(len(extent))]
    entries = entries.at[tuple(spot)].set(smallest)
    longest = extent.index(max(extent))
    spot[longest] = (spot[longest] + 1) % extent[longest]
    return entries.at[tuple(spot)].set(high)


def steps_of(key, shape, split, smallest, high):
    factor_of = 1.0
    for dim, blocks in split:
        steps = jax.random.uniform(jax.random.fold_in(jax.random.fold_in(key, 6), dim), (blocks,), jnp.float32, smallest / len(split), high / len(split))
        factor_of = factor_of * jnp.repeat(jnp.exp(steps), shape[dim] // blocks).reshape((-1,) + (1,) * (len(shape) - 1 - dim))
    return factor_of


def bell_draw(stream_key, extent, scale, most, pieces=(), kind=jnp.bfloat16):
    result = scale * jax.random.normal(stream_key, extent, jnp.float32)
    if pieces:
        result = result * steps_of(stream_key, extent, pieces, -0.22, 0.18)
    return jnp.clip(result, -most, most).astype(kind)


def setup_inputs(seed: int = 0) -> dict:
    streams_of = jax.random.split(jax.random.key(seed), 9)
    covariance = draw_covariance(jax.random.fold_in(streams_of[8], 71), 0)
    wfs_map = place_ends(jax.random.randint(streams_of[1], (M,), 0, NWFS), jax.random.fold_in(streams_of[1], 1), 0, NWFS - 1).astype(jnp.int32)
    noise_var = jnp.clip(jnp.exp(jax.random.uniform(streams_of[2], (NWFS,), jnp.float32, math.log(0.5), math.log(2.0))), 0.5, 2.0)
    targets = bell_draw(streams_of[3], (M, TC), 0.1, 0.6, ((0, 8), (1, 4)), jnp.float32)
    target_pos = jnp.clip(jax.random.uniform(streams_of[4], (2, TC), jnp.float32, -1.0, 1.0), -1.0, 1.0)
    layer_strength = jnp.clip(jnp.exp(jax.random.uniform(streams_of[5], (NL,), jnp.float32, math.log(0.005), math.log(0.05))), 0.005, 0.05)
    layer_scale = jnp.clip(jnp.exp(jax.random.uniform(streams_of[6], (NL,), jnp.float32, math.log(0.2), math.log(2.0))), 0.2, 2.0)
    tile_layer = place_ends(jax.random.randint(streams_of[7], (TC // TILE,), 0, NL), jax.random.fold_in(streams_of[7], 1), 0, NL - 1).astype(jnp.int32)
    return dict(covariance=covariance, wfs_map=wfs_map, noise_var=noise_var, targets=targets, target_pos=target_pos, layer_strength=layer_strength, layer_scale=layer_scale, tile_layer=tile_layer)


precise = lax.Precision.HIGHEST

def target_covariance(pos_rows, pos_cols, layer_rows, layer_cols, layer_strength, layer_scale):
    distance = (pos_rows[0][:, None] - pos_cols[0][None, :]) ** 2 + (pos_rows[1][:, None] - pos_cols[1][None, :]) ** 2
    lowest = jnp.minimum(layer_rows[:, None], layer_cols[None, :])
    levels = jnp.arange(layer_strength.shape[0], dtype=jnp.int32)
    weights = layer_strength[:, None, None] / (1.0 + distance[None] / (layer_scale * layer_scale)[:, None, None])
    return jnp.sum(jnp.where(levels[:, None, None] <= lowest[None], weights, 0.0), axis=0)

def reference(covariance, wfs_map, noise_var, targets, target_pos, layer_strength, layer_scale, tile_layer):
    indices = jnp.arange(M, dtype=jnp.int32)
    matrix = covariance.at[indices, indices].add(noise_var[wfs_map])
    factor = jnp.linalg.cholesky(matrix[:PB, :PB])
    solved = jax.scipy.linalg.solve_triangular(factor, matrix[:, :PB].T, lower=True).T
    top_rows = jnp.concatenate([factor, jnp.zeros((M - PB, PB), jnp.float32)], axis=0)
    panel_factor = jnp.where(indices[:, None] < PB, top_rows, solved)
    block_rows = M // 16

    def update_block(block):
        start = (block * block_rows).astype(jnp.int32)
        rows_here = lax.dynamic_slice_in_dim(panel_factor, start, block_rows, 0)
        matrix_here = lax.dynamic_slice_in_dim(matrix, start, block_rows, 0)
        row_ids = start + jnp.arange(block_rows, dtype=jnp.int32)
        product = jnp.dot(rows_here, panel_factor.T, precision=precise)
        fill_cols = jnp.concatenate([rows_here, jnp.zeros((block_rows, M - PB), jnp.float32)], axis=1)
        trailing = (row_ids[:, None] >= PB) & (indices[None, :] >= PB)
        return jnp.where(trailing, matrix_here - product, jnp.where(indices[None, :] < PB, fill_cols, 0.0))
    updated = lax.map(update_block, jnp.arange(16, dtype=jnp.int32)).reshape(M, M)
    head_rows = jax.scipy.linalg.solve_triangular(factor, targets[:PB], lower=True)
    head_top = jnp.concatenate([head_rows, jnp.zeros((M - PB, TC), jnp.float32)], axis=0)
    reduced = targets - jnp.dot(panel_factor, head_rows, precision=precise)
    reconstructor = jnp.where(indices[:, None] < PB, head_top, reduced)
    layer_all = jnp.repeat(tile_layer, TILE)

    def covariance_block(block):
        start = (block * TILE).astype(jnp.int32)
        return target_covariance(lax.dynamic_slice_in_dim(target_pos, start, TILE, 1), target_pos, lax.dynamic_slice_in_dim(layer_all, start, TILE, 0), layer_all, layer_strength, layer_scale)
    target_cov = lax.map(covariance_block, jnp.arange(TC // TILE, dtype=jnp.int32)).reshape(TC, TC)
    error_cov = target_cov - jnp.dot(head_rows.T, head_rows, precision=precise)
    return (updated, panel_factor, reconstructor, error_cov)
```

```python
import functools

import jax
import jax.numpy as jnp
from jax import lax
from jax.experimental import pallas as pl
from jax.experimental.pallas import tpu as pltpu
from jax.sharding import PartitionSpec as P

PB = 256
TILE = 128
HALF = PB // 2
STEP = 8
CHUNK = 128
ROW_CHUNKS = 12
AHEAD = 2
LATE = 2

MESH = pl.DeviceIdType.MESH
precise = lax.Precision.HIGHEST


def dot(a, b, dims=((1,), (0,))):
    return lax.dot_general(
        a, b, (dims, ((), ())), precision=precise, preferred_element_type=jnp.float32
    )


def outer(a, b):
    def thirds(x):
        high = x.astype(jnp.bfloat16).astype(jnp.float32)
        middle = (x - high).astype(jnp.bfloat16).astype(jnp.float32)
        return high, middle, x - high - middle

    p, q = thirds(a), thirds(b)
    left = jnp.concatenate([p[0], p[0], p[1], p[0], p[2], p[1]], axis=0)
    right = jnp.concatenate([q[0], q[1], q[0], q[2], q[0], q[1]], axis=0)
    return lax.dot_general(
        left.astype(jnp.bfloat16),
        right.astype(jnp.bfloat16),
        (((0,), (0,)), ((), ())),
        preferred_element_type=jnp.float32,
    )


def split(x):
    high = x.astype(jnp.bfloat16)
    return high, (x - high.astype(jnp.float32)).astype(jnp.bfloat16)


def stacked(x):
    high, low = split(x)
    return jnp.concatenate([high, high, low], axis=0)


def target_covariance(out, product, pos, strength, scale, tile_layer, row_start, col_start):
    height, width = out.shape

    def upright(axis):
        line = pos[pl.ds(axis, 1), pl.ds(row_start, height)]
        return jnp.broadcast_to(line, (TILE, height)).T

    rows = [upright(0), upright(1)]
    for i in range(height // TILE):
        for j in range(width // TILE):
            columns = pl.ds(pl.multiple_of(col_start + j * TILE, TILE), TILE)
            across = rows[0][i * TILE : (i + 1) * TILE] - pos[pl.ds(0, 1), columns]
            along = rows[1][i * TILE : (i + 1) * TILE] - pos[pl.ds(1, 1), columns]
            distance = across * across + along * along
            lowest = jnp.minimum(
                tile_layer[row_start // TILE + i], tile_layer[col_start // TILE + j]
            )

            def layer(l, total, distance=distance):
                return total + strength[l] / (1.0 + distance * (1.0 / (scale[l] * scale[l])))

            total = lax.fori_loop(0, lowest + 1, layer, jnp.zeros_like(distance))
            here = (pl.ds(i * TILE, TILE), pl.ds(j * TILE, TILE))
            out[here] = total - product[here]


def gray_neighbours(c, n):
    position = c * 0
    after = c * 0
    before = c * 0
    ring = [i ^ (i >> 1) for i in range(n)]
    for i, node in enumerate(ring):
        position = jnp.where(c == node, i, position)
        after = jnp.where(c == node, ring[(i + 1) % n], after)
        before = jnp.where(c == node, ring[(i - 1) % n], before)
    return position, after, before


def pivot_step(t_ref, i):
    n = t_ref.shape[0]
    lanes = lax.broadcasted_iota(jnp.int32, (8, n), 1)
    wide = lax.broadcasted_iota(jnp.int32, (8, 2 * n), 1)
    down = lax.broadcasted_iota(jnp.int32, (8, 1), 0)
    k = pl.multiple_of(i * 8, 8)
    rows = t_ref[pl.ds(k, 8), :]
    left = rows[:, :n]
    columns = [
        jnp.sum(jnp.where(lanes == k + j, left, 0.0), axis=1, keepdims=True) for j in range(8)
    ]
    scale = jnp.ones((8, 1), jnp.float32)
    for j in range(8):
        pivot = columns[j][j : j + 1]
        scale = jnp.where(down == j, lax.rsqrt(pivot), scale)
        if j < 7:
            factor = jnp.where(down > j, columns[j] * (1.0 / pivot), 0.0)
            rows = rows - factor * rows[j : j + 1]
            for later in range(j + 1, 8):
                columns[later] = columns[later] - factor * columns[later][j : j + 1]
    rows = rows * scale
    rows = jnp.where((wide >= n) | (wide >= k + down), rows, 0.0)
    below = jnp.where(lanes >= k + 8, rows[:, :n], 0.0)
    t_ref[...] = t_ref[...] - outer(below, rows)
    t_ref[pl.ds(k, 8), :] = rows


def run(condition, action):
    @pl.when(condition)
    def _():
        action()


def panel_kernel(
    n_row,
    n_col,
    cov,
    targets,
    sensors,
    noise_var,
    updated,
    reconstructor,
    panel,
    product,
    row_raw,
    col_raw,
    need_raw,
    blocks,
    head_sensors,
    own_sensors,
    kinds,
    noise,
    t_ref,
    factor_ref,
    inverse_ref,
    parts,
    solver,
    local_sem,
    cov_sem,
    diag_send,
    diag_recv,
    col_send,
    col_recv,
    row_send,
    row_recv,
    need_send,
    need_recv,
):
    r = lax.axis_index("row")
    c = lax.axis_index("col")
    row_count, col_count = updated.shape
    width = reconstructor.shape[1]
    need = need_raw.shape[1]
    pairs = col_count // PB
    head_chunks = width // CHUNK
    chunks = head_chunks + col_count // CHUNK
    even = lax.rem(r, 2) == 0
    plane = lax.div(r, 2)
    place, after, before = gray_neighbours(c, n_col)
    far_row = jnp.minimum(r + 2, n_row - 1)
    near_row = jnp.where(even, r + 1, r - 1)
    has_far = even & (r + 2 < n_row)
    has_near = even & (r + 1 < n_row)
    relays = even & (r > 0)
    first = (r == 0) & (c == 0)
    half_ring = n_col // 2

    head_span = pl.ds(0, width)
    head_copy = pltpu.make_async_copy(
        targets.at[pl.ds(0, PB), :], col_raw.at[:, head_span], local_sem.at[0]
    )
    col_copy = pltpu.make_async_copy(
        cov.at[pl.ds(0, PB), :], col_raw.at[:, pl.ds(width, col_count)], local_sem.at[1]
    )
    row_copy = pltpu.make_async_copy(cov.at[:, pl.ds(0, PB)], row_raw, local_sem.at[2])
    target_copy = pltpu.make_async_copy(targets, reconstructor, local_sem.at[3])
    sensor_copy = pltpu.make_async_copy(sensors, own_sensors, local_sem.at[9])
    noise_copy = pltpu.make_async_copy(noise_var, kinds, local_sem.at[10])
    quarters = [(0, 0), (HALF, 0), (HALF, HALF)]

    def diag_piece(i, source):
        if i == 0:
            return (sensors.at[pl.ds(0, PB)] if source else head_sensors), head_sensors
        dst = blocks.at[i - 1]
        if source:
            y, x = quarters[i - 1]
            return cov.at[pl.ds(y, HALF), pl.ds(x, HALF)], dst
        return dst, dst

    own_diag = [
        pltpu.make_async_copy(*diag_piece(i, True), local_sem.at[5 + i]) for i in range(4)
    ]

    def cov_copy(p):
        columns = pl.ds(pl.multiple_of(p * PB, PB), PB)
        return pltpu.make_async_copy(cov.at[:, columns], updated.at[:, columns], cov_sem.at[p])

    for copy in own_diag:
        run(first, copy.start)
    sensor_copy.start()
    noise_copy.start()

    barrier = pltpu.get_barrier_semaphore()

    def greet(col, row):
        pl.semaphore_signal(barrier, inc=1, device_id=(col, row), device_id_type=MESH)

    greet(c, near_row)
    for k in range(1, n_col):
        greet(lax.rem(c + k, n_col), r)
    run(has_far, lambda: greet(c, far_row))
    run(relays, lambda: greet(c, jnp.maximum(r - 2, 0)))
    pl.semaphore_wait(barrier, n_col + jnp.where(has_far, 1, 0) + jnp.where(relays, 1, 0))

    def remote(src, dst, send, recv, col, row):
        return pltpu.make_async_remote_copy(
            src_ref=src,
            dst_ref=dst,
            send_sem=send,
            recv_sem=recv,
            device_id=(col, row),
            device_id_type=MESH,
        )

    def upward(src, dst, send, recv):
        return (
            remote(src, dst, send[0], recv, c, far_row),
            remote(src, dst, send[1], recv, c, near_row),
        )

    def diag_copies(i, source):
        src, dst = diag_piece(i, source)
        ring = [
            remote(src, dst, diag_send.at[i, k], diag_recv.at[i], to, r)
            for k, to in enumerate([after, before])
        ]
        return ring, upward(src, dst, [diag_send.at[i, 2], diag_send.at[i, 3]], diag_recv.at[i])

    ring_after = (r == 0) & (place < half_ring)
    ring_before = (r == 0) & ((place == 0) | (place >= half_ring + 2))

    def diag_each(i, source, allowed, what):
        ring, up = diag_copies(i, source)
        run(allowed & has_far, lambda: what(up[0]))
        run(allowed & has_near, lambda: what(up[1]))
        run(allowed & ring_after, lambda: what(ring[0]))
        run(allowed & ring_before, lambda: what(ring[1]))

    def start(copy):
        copy.start()

    def finish(copy):
        copy.wait_send()

    def span(q):
        return pl.ds(pl.multiple_of(q * CHUNK, CHUNK), CHUNK)

    def chunk_copies(q, src):
        return upward(
            src, col_raw.at[:, span(q)], [col_send.at[q, 0], col_send.at[q, 1]], col_recv.at[q]
        )

    def chunk_start(copies):
        run(has_far, copies[0].start)
        run(has_near, copies[1].start)

    def source_chunk(q):
        run(
            q < head_chunks,
            lambda: chunk_start(
                chunk_copies(q, targets.at[pl.ds(0, PB), span(jnp.minimum(q, head_chunks - 1))])
            ),
        )
        run(
            q >= head_chunks,
            lambda: chunk_start(
                chunk_copies(q, cov.at[pl.ds(0, PB), span(jnp.maximum(q - head_chunks, 0))])
            ),
        )

    def each(low, high, action):
        def body(i, carry):
            action(i)
            return carry

        lax.fori_loop(low, high, body, 0)

    def chunk_take(q):
        copies = chunk_copies(q, col_raw.at[:, span(q)])
        copies[0].wait_recv()
        run(even, lambda: chunk_start(copies))

    def takes(low, high):
        run(relays, lambda: each(low, high, chunk_take))

    step_rows = row_count // (2 * ROW_CHUNKS)

    def row_copies(j, way, source):
        rows = pl.ds(pl.multiple_of((2 * j + way) * step_rows, step_rows), step_rows)
        dst = row_raw.at[rows, :]
        src = cov.at[rows, pl.ds(0, PB)] if source else dst
        to = after if way == 0 else before
        return remote(src, dst, row_send.at[j, way], row_recv.at[j, way], to, r)

    def forwards(way):
        return (place > 0) & ((place < n_col - 1) if way == 0 else (place > 1))

    def row_source(j):
        for way in range(2):
            row_copies(j, way, True).start()

    def row_forward(j):
        for way in range(2):
            copy = row_copies(j, way, False)
            run(forwards(way), lambda: (copy.wait_recv(), copy.start()))

    def diag_pass(i):
        run((r > 0) | (c > 0), diag_copies(i, False)[0][0].wait_recv)
        diag_each(i, False, ~first, start)
        run(first, own_diag[i].wait)

    def noise_of(sensor):
        total = jnp.zeros(sensor.shape, jnp.float32)
        for k in range(noise_var.shape[0]):
            total = jnp.where(sensor == k, kinds[k], total)
        return total

    def row_goal(s):
        late = jnp.where(place == half_ring, 7, 2) + jnp.where(plane == 0, 3, 0)
        return jnp.clip(lax.div(jnp.maximum(s + 4 * plane - late, 0), 3), 0, ROW_CHUNKS)

    for i in range(4):
        diag_each(i, True, first, start)
    run((r == 0) & (c > 0), lambda: each(0, AHEAD, source_chunk))
    run((place == 0) & ((r == 0) | (r > 1)), lambda: each(0, ROW_CHUNKS, row_source))
    run(first, lambda: each(0, chunks, source_chunk))
    run(c > 0, lambda: takes(0, AHEAD))
    each(0, row_goal(-1), row_forward)
    diag_pass(0)
    diag_pass(1)
    sensor_copy.wait()
    noise_copy.wait()
    noise[...] = noise_of(own_sensors[...].reshape(1, row_count))
    head_noise = noise_of(head_sensors[...].reshape(1, PB))
    unit = lax.broadcasted_iota(jnp.int32, (HALF, HALF), 0) == lax.broadcasted_iota(
        jnp.int32, (HALF, HALF), 1
    )

    def chunk_goal(s):
        late = jnp.where(c == 0, 5, 1)
        return jnp.maximum(lax.div(jnp.maximum(s - late, 0), 3), jnp.where(c == 0, 0, AHEAD))

    steps = HALF // STEP

    def side_work(s):
        @pl.when(s == 2)
        def _():
            diag_pass(2)

        @pl.when(s == 4)
        def _():
            diag_pass(3)
            run((place == 0) & (r == 1), lambda: each(0, ROW_CHUNKS, row_source))
            run((r == 0) & (c > 0), lambda: each(AHEAD, chunks, source_chunk))

        @pl.when(s == 6)
        def _():
            run(r == 0, lambda: (head_copy.start(), col_copy.start()))
            run(c == 0, row_copy.start)

        run(s == 8, target_copy.start)
        run((lax.rem(s, 2) == 1) & (lax.div(s, 2) < pairs), lambda: cov_copy(lax.div(s, 2)).start())
        takes(chunk_goal(s - 1), chunk_goal(s))
        each(row_goal(s - 1), row_goal(s), row_forward)

    def half(block, where):
        t_ref[:, pl.ds(0, HALF)] = block
        t_ref[:, pl.ds(HALF, HALF)] = unit.astype(jnp.float32)

        def step(i, carry):
            pivot_step(t_ref, i)
            side_work(i + where * steps)
            return carry

        lax.fori_loop(0, steps, step, 0)

    owner = lax.div(r * need, width)
    offset = pl.multiple_of(lax.rem(r * need, width), CHUNK)
    need_copies = [
        remote(col_raw.at[:, pl.ds(offset, need)], need_raw, need_send.at[k], need_recv, k, r)
        for k in range(n_col)
    ]
    own_need = pltpu.make_async_copy(
        col_raw.at[:, pl.ds(offset, need)], need_raw, local_sem.at[4]
    )

    def need_start():
        run(r == 0, head_copy.wait)
        run(~even, lambda: each(0, head_chunks, chunk_take))
        for k in range(n_col):
            run((c == owner) & (c != k), need_copies[k].start)
        run(c == owner, own_need.start)

    half(blocks[0] + jnp.where(unit, head_noise[:, :HALF], 0.0), 0)
    inverse_11 = t_ref[:, pl.ds(HALF, HALF)]
    inverse_ref[pl.ds(0, HALF), pl.ds(0, HALF)] = inverse_11
    inverse_ref[pl.ds(0, HALF), pl.ds(HALF, HALF)] = jnp.zeros((HALF, HALF), jnp.float32)
    factor_ref[pl.ds(0, HALF), pl.ds(0, HALF)] = t_ref[:, pl.ds(0, HALF)].T
    factor_ref[pl.ds(0, HALF), pl.ds(HALF, HALF)] = jnp.zeros((HALF, HALF), jnp.float32)
    lower = dot(blocks[1], inverse_11, ((1,), (1,)))
    factor_ref[pl.ds(HALF, HALF), pl.ds(0, HALF)] = lower
    half(
        blocks[2]
        + jnp.where(unit, head_noise[:, HALF:], 0.0)
        - dot(lower, lower, ((1,), (1,))),
        1,
    )
    inverse_22 = t_ref[:, pl.ds(HALF, HALF)]
    inverse_ref[pl.ds(HALF, HALF), pl.ds(HALF, HALF)] = inverse_22
    factor_ref[pl.ds(HALF, HALF), pl.ds(HALF, HALF)] = t_ref[:, pl.ds(0, HALF)].T
    lower = factor_ref[pl.ds(HALF, HALF), pl.ds(0, HALF)]
    inverse_ref[pl.ds(HALF, HALF), pl.ds(0, HALF)] = -dot(
        inverse_22, dot(lower, inverse_ref[pl.ds(0, HALF), pl.ds(0, HALF)])
    )
    last = 2 * steps - 1
    each(row_goal(last), ROW_CHUNKS, row_forward)
    goal = chunk_goal(last)
    takes(goal, goal + LATE)
    goal = goal + LATE

    inverse = inverse_ref[...]
    solver[:, pl.ds(0, PB)] = stacked(inverse.T)
    solver[:, pl.ds(PB, PB)] = stacked(dot(inverse, inverse, ((0,), (0,))))

    def row_wait(j):
        for way in range(2):
            run((place > 0) & ~forwards(way), row_copies(j, way, False).wait_recv)

    each(0, ROW_CHUNKS, row_wait)
    run(c == 0, row_copy.wait)
    takes(goal, goal + 1)
    goal = goal + 1
    need_start()
    each(min(2 * steps // 2, pairs), pairs, lambda p: cov_copy(p).start())

    def solve(i, carry):
        rows = pl.ds(pl.multiple_of(i * PB, PB), PB)
        high, low = split(row_raw[rows, :])
        both = jnp.dot(
            jnp.concatenate([high, low, high], axis=1),
            solver[...],
            preferred_element_type=jnp.float32,
        )
        panel[rows, :] = both[:, :PB]
        high, low = split(both[:, PB:])
        parts[rows, pl.ds(0, PB)] = high
        parts[rows, pl.ds(PB, PB)] = low
        parts[rows, pl.ds(2 * PB, PB)] = high
        return carry

    lax.fori_loop(0, row_count // PB, solve, 0)

    @pl.when(r == 0)
    def _():
        panel[pl.ds(0, PB), :] = factor_ref[...]

    takes(goal, goal + 1)
    goal = goal + 1

    head = dot(inverse, col_raw[:, head_span])
    target_copy.wait()
    reconstructor[...] = reconstructor[...] - jnp.dot(
        parts[...], stacked(col_raw[:, head_span]), preferred_element_type=jnp.float32
    )

    @pl.when(r == 0)
    def _():
        reconstructor[pl.ds(0, PB), :] = head

    run(r == 0, col_copy.wait)

    def reach(p):
        return jnp.minimum(jnp.maximum(goal + p, head_chunks + 2 * p), chunks)

    def update(p):
        takes(reach(p), reach(p + 1))
        run(
            ~even,
            lambda: each(head_chunks + 2 * p, head_chunks + 2 * p + 2, chunk_take),
        )
        cov_copy(p).wait()
        columns = pl.ds(pl.multiple_of(p * PB, PB), PB)
        raw = col_raw[:, pl.ds(pl.multiple_of(width + p * PB, CHUNK), PB)]
        updated[:, columns] = updated[:, columns] - jnp.dot(
            parts[...], stacked(raw), preferred_element_type=jnp.float32
        )
        begin = c * col_count + p * PB - r * row_count

        @pl.when((begin >= 0) & (begin < row_count))
        def _():
            block = pl.ds(pl.multiple_of(begin, PB), PB)
            diagonal = lax.broadcasted_iota(jnp.int32, (PB, PB), 0) == (
                lax.broadcasted_iota(jnp.int32, (PB, PB), 1)
            )
            updated[block, columns] = updated[block, columns] + jnp.where(
                diagonal, noise[:, block], 0.0
            )

        @pl.when(r == 0)
        def _():
            updated[pl.ds(0, PB), columns] = jnp.zeros((PB, PB), jnp.float32)

    def finish_product():
        run(c == owner, own_need.wait)
        run(c != owner, need_copies[0].wait_recv)
        product[...] = dot(dot(inverse, need_raw[...]), head, ((0,), (0,)))

    tail = pairs - pairs // 6
    each(0, tail, update)
    finish_product()
    each(tail, pairs, update)

    @pl.when(c == 0)
    def _():
        updated[:, pl.ds(0, PB)] = panel[...]

    for k in range(n_col):
        run((c == owner) & (c != k), need_copies[k].wait_send)
    for i in range(4):
        diag_each(i, False, r >= 0, finish)

    def chunk_finish(q):
        copies = chunk_copies(q, col_raw.at[:, span(q)])
        run(has_far, copies[0].wait_send)
        run(has_near, copies[1].wait_send)

    each(0, chunks, chunk_finish)

    def row_finish(j):
        for way in range(2):
            run((place == 0) | forwards(way), row_copies(j, way, False).wait_send)

    each(0, ROW_CHUNKS, row_finish)


SLABS = 6


def store_kernel(
    updated,
    reconstructor,
    panel,
    product,
    pos,
    strength,
    scale,
    tile_layer,
    updated_out,
    reconstructor_out,
    panel_out,
    error_out,
    error,
    sems,
):
    r = lax.axis_index("row")
    c = lax.axis_index("col")
    slab = updated.shape[0] // SLABS
    copies = [
        pltpu.make_async_copy(
            updated.at[pl.ds(i * slab, slab), :],
            updated_out.at[pl.ds(i * slab, slab), :],
            sems.at[i],
        )
        for i in range(SLABS)
    ]
    copies.append(pltpu.make_async_copy(reconstructor, reconstructor_out, sems.at[SLABS]))
    copies.append(pltpu.make_async_copy(panel, panel_out, sems.at[SLABS + 1]))
    for copy in copies:
        copy.start()
    height, width = error.shape
    target_covariance(
        error,
        product,
        pos,
        strength,
        scale,
        tile_layer,
        pl.multiple_of(r * height, TILE),
        pl.multiple_of(c * width, TILE),
    )
    last = pltpu.make_async_copy(error, error_out, sems.at[SLABS + 2])
    last.start()
    for copy in copies:
        copy.wait()
    last.wait()


def local(
    n_row, n_col, covariance, wfs_map, noise_var, targets, target_pos, layer_strength,
    layer_scale, tile_layer
):
    row_count, col_count = covariance.shape
    target_width = targets.shape[1]
    error_rows = target_width * n_col // n_row
    chunks = (target_width + col_count) // CHUNK

    def f32(*shape):
        return jax.ShapeDtypeStruct(shape, jnp.float32)

    vmem = pl.BlockSpec(memory_space=pltpu.VMEM)
    anywhere = pl.BlockSpec(memory_space=pltpu.HBM)
    smem = pl.BlockSpec(memory_space=pltpu.SMEM)
    dma = pltpu.SemaphoreType.DMA
    results = pl.pallas_call(
        functools.partial(panel_kernel, n_row, n_col),
        out_shape=(
            f32(row_count, col_count),
            f32(row_count, target_width),
            f32(row_count, PB),
            f32(error_rows, target_width),
        ),
        in_specs=[anywhere] * 4,
        out_specs=[vmem] * 4,
        scratch_shapes=[
            pltpu.VMEM((row_count, PB), jnp.float32),
            pltpu.VMEM((PB, target_width + col_count), jnp.float32),
            pltpu.VMEM((PB, error_rows), jnp.float32),
            pltpu.VMEM((3, HALF, HALF), jnp.float32),
            pltpu.VMEM((PB,), jnp.int32),
            pltpu.VMEM((row_count,), jnp.int32),
            pltpu.SMEM(noise_var.shape, jnp.float32),
            pltpu.VMEM((1, row_count), jnp.float32),
            pltpu.VMEM((HALF, PB), jnp.float32),
            pltpu.VMEM((PB, PB), jnp.float32),
            pltpu.VMEM((PB, PB), jnp.float32),
            pltpu.VMEM((row_count, 3 * PB), jnp.bfloat16),
            pltpu.VMEM((3 * PB, 2 * PB), jnp.bfloat16),
            dma((11,)),
            dma((col_count // PB,)),
            dma((4, 4)),
            dma((4,)),
            dma((chunks, 2)),
            dma((chunks,)),
            dma((ROW_CHUNKS, 2)),
            dma((ROW_CHUNKS, 2)),
            dma((n_col,)),
            dma,
        ],
        compiler_params=pltpu.CompilerParams(
            collective_id=0, has_side_effects=True, vmem_limit_bytes=16 * 1024 * 1024
        ),
        name="panel",
    )(
        covariance,
        *[pltpu.with_memory_space_constraint(x, pltpu.HBM) for x in (targets, wfs_map, noise_var)],
    )

    outs = pl.pallas_call(
        store_kernel,
        out_shape=(
            f32(row_count, col_count),
            f32(row_count, target_width),
            f32(row_count, PB),
            f32(error_rows, target_width),
        ),
        in_specs=[vmem] * 5 + [smem] * 3,
        out_specs=[anywhere] * 4,
        scratch_shapes=[pltpu.VMEM((error_rows, target_width), jnp.float32), dma((SLABS + 3,))],
        compiler_params=pltpu.CompilerParams(vmem_limit_bytes=4 * 1024 * 1024),
        name="store",
    )(*results, target_pos, layer_strength, layer_scale, tile_layer)
    updated, reconstructor, panel, error_cov = outs
    return updated, panel, reconstructor, error_cov


def solution(mesh):
    placed = (P("row", "col"), P("row"), P(), P("row", "col"), P(), P(), P(), P())
    return jax.shard_map(
        functools.partial(local, mesh.shape["row"], mesh.shape["col"]),
        mesh=mesh,
        in_specs=placed,
        out_specs=(P("row", "col"), P("row", None), P("row", "col"), P("row", "col")),
        check_vma=False,
    )
```

```python
import functools

import jax
import jax.numpy as jnp
from jax import lax
from jax.experimental import pallas as pl
from jax.experimental.pallas import tpu as pltpu
from jax.sharding import PartitionSpec as P

PB = 256
TILE = 128
HALF = PB // 2
STEP = 8
CHUNK = 128
GROUP = 4
ROW_CHUNKS = 12
AHEAD = 3
LATE = 3

MESH = pl.DeviceIdType.MESH
precise = lax.Precision.HIGHEST


def dot(a, b, dims=((1,), (0,))):
    return lax.dot_general(
        a, b, (dims, ((), ())), precision=precise, preferred_element_type=jnp.float32
    )


def outer(a, b):
    def thirds(x):
        high = x.astype(jnp.bfloat16).astype(jnp.float32)
        middle = (x - high).astype(jnp.bfloat16).astype(jnp.float32)
        return high, middle, x - high - middle

    p, q = thirds(a), thirds(b)
    left = jnp.concatenate([p[0], p[0], p[1], p[0], p[2], p[1]], axis=0)
    right = jnp.concatenate([q[0], q[1], q[0], q[2], q[0], q[1]], axis=0)
    return lax.dot_general(
        left.astype(jnp.bfloat16),
        right.astype(jnp.bfloat16),
        (((0,), (0,)), ((), ())),
        preferred_element_type=jnp.float32,
    )


def split(x):
    high = x.astype(jnp.bfloat16)
    return high, (x - high.astype(jnp.float32)).astype(jnp.bfloat16)


def stacked(x):
    high, low = split(x)
    return jnp.concatenate([high, high, low], axis=0)


def target_covariance(out, product, pos, strength, scale, tile_layer, row_start, col_start):
    height, width = out.shape
    levels = strength.shape[0]

    def upright(axis):
        line = pos[pl.ds(axis, 1), pl.ds(row_start, height)]
        return jnp.broadcast_to(line, (TILE, height)).T

    rows = [upright(0), upright(1)]
    for i in range(height // TILE):
        for j in range(width // TILE):
            columns = pl.ds(pl.multiple_of(col_start + j * TILE, TILE), TILE)
            across = rows[0][i * TILE : (i + 1) * TILE] - pos[pl.ds(0, 1), columns]
            along = rows[1][i * TILE : (i + 1) * TILE] - pos[pl.ds(1, 1), columns]
            distance = across * across + along * along
            lowest = jnp.minimum(
                tile_layer[row_start // TILE + i], tile_layer[col_start // TILE + j]
            )

            def layers(g, total, distance=distance, lowest=lowest):
                terms = []
                for k in range(GROUP):
                    l = jnp.minimum(g * GROUP + k, levels - 1)
                    weight = jnp.where(g * GROUP + k <= lowest, strength[l], 0.0)
                    square = scale[l] * scale[l]
                    terms.append((weight * square, square + distance))
                while len(terms) > 1:
                    terms = [
                        (a[0] * b[1] + b[0] * a[1], a[1] * b[1])
                        for a, b in zip(terms[::2], terms[1::2])
                    ]
                return total + terms[0][0] / terms[0][1]

            total = lax.fori_loop(0, lax.div(lowest, GROUP) + 1, layers, jnp.zeros_like(distance))
            here = (pl.ds(i * TILE, TILE), pl.ds(j * TILE, TILE))
            out[here] = total - product[here]


def gray_neighbours(c, n):
    position = c * 0
    after = c * 0
    before = c * 0
    ring = [i ^ (i >> 1) for i in range(n)]
    for i, node in enumerate(ring):
        position = jnp.where(c == node, i, position)
        after = jnp.where(c == node, ring[(i + 1) % n], after)
        before = jnp.where(c == node, ring[(i - 1) % n], before)
    return position, after, before


def pivot_step(t_ref, i):
    n = t_ref.shape[0]
    lanes = lax.broadcasted_iota(jnp.int32, (8, n), 1)
    wide = lax.broadcasted_iota(jnp.int32, (8, 2 * n), 1)
    down = lax.broadcasted_iota(jnp.int32, (8, 1), 0)
    k = pl.multiple_of(i * 8, 8)
    rows = t_ref[pl.ds(k, 8), :]
    left = rows[:, :n]
    columns = [
        jnp.sum(jnp.where(lanes == k + j, left, 0.0), axis=1, keepdims=True) for j in range(8)
    ]
    scale = jnp.ones((8, 1), jnp.float32)
    for j in range(8):
        pivot = columns[j][j : j + 1]
        scale = jnp.where(down == j, lax.rsqrt(pivot), scale)
        if j < 7:
            factor = jnp.where(down > j, columns[j] * (1.0 / pivot), 0.0)
            rows = rows - factor * rows[j : j + 1]
            for later in range(j + 1, 8):
                columns[later] = columns[later] - factor * columns[later][j : j + 1]
    rows = rows * scale
    rows = jnp.where((wide >= n) | (wide >= k + down), rows, 0.0)
    below = jnp.where(lanes >= k + 8, rows[:, :n], 0.0)
    t_ref[...] = t_ref[...] - outer(below, rows)
    t_ref[pl.ds(k, 8), :] = rows


def run(condition, action):
    @pl.when(condition)
    def _():
        action()


def panel_kernel(
    n_row,
    n_col,
    cov,
    targets,
    sensors,
    noise_var,
    updated,
    reconstructor,
    panel,
    product,
    row_raw,
    col_raw,
    need_raw,
    blocks,
    head_sensors,
    own_sensors,
    kinds,
    noise,
    t_ref,
    factor_ref,
    inverse_ref,
    parts,
    solver,
    head_ref,
    local_sem,
    cov_sem,
    diag_send,
    diag_recv,
    col_send,
    col_recv,
    row_send,
    row_recv,
    need_send,
    need_recv,
):
    r = lax.axis_index("row")
    c = lax.axis_index("col")
    row_count, col_count = updated.shape
    width = reconstructor.shape[1]
    need = need_raw.shape[1]
    pairs = col_count // PB
    head_chunks = width // CHUNK
    chunks = head_chunks + col_count // CHUNK
    even = lax.rem(r, 2) == 0
    plane = lax.div(r, 2)
    place, after, before = gray_neighbours(c, n_col)
    far_row = jnp.minimum(r + 2, n_row - 1)
    near_row = jnp.where(even, r + 1, r - 1)
    has_far = even & (r + 2 < n_row)
    has_near = even & (r + 1 < n_row)
    relays = even & (r > 0)
    first = (r == 0) & (c == 0)
    half_ring = n_col // 2
    ahead = jnp.where(place == half_ring, AHEAD + 2, AHEAD)

    head_span = pl.ds(0, width)
    head_copy = pltpu.make_async_copy(
        targets.at[pl.ds(0, PB), :], col_raw.at[:, head_span], local_sem.at[0]
    )
    col_copy = pltpu.make_async_copy(
        cov.at[pl.ds(0, PB), :], col_raw.at[:, pl.ds(width, col_count)], local_sem.at[1]
    )
    row_copy = pltpu.make_async_copy(cov.at[:, pl.ds(0, PB)], row_raw, local_sem.at[2])
    target_copy = pltpu.make_async_copy(targets, reconstructor, local_sem.at[3])
    sensor_copy = pltpu.make_async_copy(sensors, own_sensors, local_sem.at[9])
    noise_copy = pltpu.make_async_copy(noise_var, kinds, local_sem.at[10])
    quarters = [(0, 0), (HALF, 0), (HALF, HALF)]

    def diag_piece(i, source):
        if i == 0:
            return (sensors.at[pl.ds(0, PB)] if source else head_sensors), head_sensors
        dst = blocks.at[i - 1]
        if source:
            y, x = quarters[i - 1]
            return cov.at[pl.ds(y, HALF), pl.ds(x, HALF)], dst
        return dst, dst

    own_diag = [
        pltpu.make_async_copy(*diag_piece(i, True), local_sem.at[5 + i]) for i in range(4)
    ]

    def cov_copy(p):
        columns = pl.ds(pl.multiple_of(p * PB, PB), PB)
        return pltpu.make_async_copy(cov.at[:, columns], updated.at[:, columns], cov_sem.at[p])

    for copy in own_diag:
        run(first, copy.start)
    sensor_copy.start()
    noise_copy.start()

    barrier = pltpu.get_barrier_semaphore()

    def greet(col, row):
        pl.semaphore_signal(barrier, inc=1, device_id=(col, row), device_id_type=MESH)

    greet(c, near_row)
    for k in range(1, n_col):
        greet(lax.rem(c + k, n_col), r)
    run(has_far, lambda: greet(c, far_row))
    run(relays, lambda: greet(c, jnp.maximum(r - 2, 0)))
    pl.semaphore_wait(barrier, n_col + jnp.where(has_far, 1, 0) + jnp.where(relays, 1, 0))

    def remote(src, dst, send, recv, col, row):
        return pltpu.make_async_remote_copy(
            src_ref=src,
            dst_ref=dst,
            send_sem=send,
            recv_sem=recv,
            device_id=(col, row),
            device_id_type=MESH,
        )

    def upward(src, dst, send, recv):
        return (
            remote(src, dst, send[0], recv, c, far_row),
            remote(src, dst, send[1], recv, c, near_row),
        )

    def diag_copies(i, source):
        src, dst = diag_piece(i, source)
        ring = [
            remote(src, dst, diag_send.at[i, k], diag_recv.at[i], to, r)
            for k, to in enumerate([after, before])
        ]
        return ring, upward(src, dst, [diag_send.at[i, 2], diag_send.at[i, 3]], diag_recv.at[i])

    ring_after = (r == 0) & (place < half_ring)
    ring_before = (r == 0) & ((place == 0) | (place >= half_ring + 2))

    def diag_each(i, source, allowed, what):
        ring, up = diag_copies(i, source)
        run(allowed & has_far, lambda: what(up[0]))
        run(allowed & has_near, lambda: what(up[1]))
        run(allowed & ring_after, lambda: what(ring[0]))
        run(allowed & ring_before, lambda: what(ring[1]))

    def start(copy):
        copy.start()

    def finish(copy):
        copy.wait_send()

    def span(q):
        return pl.ds(pl.multiple_of(q * CHUNK, CHUNK), CHUNK)

    def chunk_copies(q, src):
        return upward(
            src, col_raw.at[:, span(q)], [col_send.at[q, 0], col_send.at[q, 1]], col_recv.at[q]
        )

    def chunk_start(copies):
        run(has_far, copies[0].start)
        run(has_near, copies[1].start)

    def source_chunk(q):
        run(
            q < head_chunks,
            lambda: chunk_start(
                chunk_copies(q, targets.at[pl.ds(0, PB), span(jnp.minimum(q, head_chunks - 1))])
            ),
        )
        run(
            q >= head_chunks,
            lambda: chunk_start(
                chunk_copies(q, cov.at[pl.ds(0, PB), span(jnp.maximum(q - head_chunks, 0))])
            ),
        )

    def each(low, high, action):
        def body(i, carry):
            action(i)
            return carry

        lax.fori_loop(low, high, body, 0)

    def chunk_take(q):
        copies = chunk_copies(q, col_raw.at[:, span(q)])
        copies[0].wait_recv()
        run(even, lambda: chunk_start(copies))

    def takes(low, high):
        run(relays, lambda: each(low, high, chunk_take))

    step_rows = row_count // (2 * ROW_CHUNKS)

    def row_copies(j, way, source):
        rows = pl.ds(pl.multiple_of((2 * j + way) * step_rows, step_rows), step_rows)
        dst = row_raw.at[rows, :]
        src = cov.at[rows, pl.ds(0, PB)] if source else dst
        to = after if way == 0 else before
        return remote(src, dst, row_send.at[j, way], row_recv.at[j, way], to, r)

    def forwards(way):
        return (place > 0) & ((place < n_col - 1) if way == 0 else (place > 1))

    def row_source(j):
        for way in range(2):
            row_copies(j, way, True).start()

    def row_forward(j):
        for way in range(2):
            copy = row_copies(j, way, False)
            run(forwards(way), lambda: (copy.wait_recv(), copy.start()))

    def diag_pass(i):
        run((r > 0) | (c > 0), diag_copies(i, False)[0][0].wait_recv)
        diag_each(i, False, ~first, start)
        run(first, own_diag[i].wait)

    def noise_of(sensor):
        total = jnp.zeros(sensor.shape, jnp.float32)
        for k in range(noise_var.shape[0]):
            total = jnp.where(sensor == k, kinds[k], total)
        return total

    def row_goal(s):
        late = jnp.where(place == half_ring, 1, 0) + jnp.where(plane == 0, 3, -1)
        reach = lax.div(jnp.maximum(s + lax.div(14 * plane, 3) - late, 0), 3)
        return jnp.minimum(reach, ROW_CHUNKS)

    for i in range(4):
        diag_each(i, True, first, start)
    run((r == 0) & (c > 0), lambda: each(0, ahead, source_chunk))
    run((place == 0) & (r != 1), lambda: each(0, ROW_CHUNKS, row_source))
    run(first, lambda: each(0, chunks, source_chunk))
    run(c > 0, lambda: takes(0, ahead))
    early_rows = jnp.maximum(row_goal(-1) - 1, 0)
    each(0, early_rows, row_forward)
    diag_pass(0)
    diag_pass(1)
    run((place == 0) & (r == 1), lambda: each(0, ROW_CHUNKS, row_source))
    sensor_copy.wait()
    noise_copy.wait()
    noise[...] = noise_of(own_sensors[...].reshape(1, row_count))
    head_noise = noise_of(head_sensors[...].reshape(1, PB))
    unit = lax.broadcasted_iota(jnp.int32, (HALF, HALF), 0) == lax.broadcasted_iota(
        jnp.int32, (HALF, HALF), 1
    )

    def chunk_goal(s):
        early = jnp.where(has_far, jnp.where(c == 0, -1, 7), -3)
        return jnp.maximum(lax.div(jnp.maximum(s + early, 0), 3), jnp.where(c == 0, 0, ahead))

    steps = HALF // STEP

    def side_work(s):
        @pl.when(s == 2)
        def _():
            diag_pass(2)

        @pl.when(s == 4)
        def _():
            diag_pass(3)
            run((r == 0) & (c > 0), lambda: each(ahead, chunks, source_chunk))

        @pl.when(s == 6)
        def _():
            run(r == 0, lambda: (head_copy.start(), col_copy.start()))
            run(c == 0, row_copy.start)

        run(s == 8, target_copy.start)
        run((lax.rem(s, 2) == 1) & (lax.div(s, 2) < pairs), lambda: cov_copy(lax.div(s, 2)).start())
        takes(chunk_goal(s - 1), chunk_goal(s))
        each(jnp.where(s > 0, row_goal(s - 1), early_rows), row_goal(s), row_forward)

    def half(block, where):
        t_ref[:, pl.ds(0, HALF)] = block
        t_ref[:, pl.ds(HALF, HALF)] = unit.astype(jnp.float32)

        def step(i, carry):
            pivot_step(t_ref, i)
            side_work(i + where * steps)
            return carry

        lax.fori_loop(0, steps, step, 0)

    owner = lax.div(r * need, width)
    offset = pl.multiple_of(lax.rem(r * need, width), CHUNK)
    need_copies = [
        remote(col_raw.at[:, pl.ds(offset, need)], need_raw, need_send.at[k], need_recv, k, r)
        for k in range(n_col)
    ]
    own_need = pltpu.make_async_copy(
        col_raw.at[:, pl.ds(offset, need)], need_raw, local_sem.at[4]
    )

    def need_start():
        for k in range(n_col):
            run((c == owner) & (c != k), need_copies[k].start)
        run(c == owner, own_need.start)

    half(blocks[0] + jnp.where(unit, head_noise[:, :HALF], 0.0), 0)
    inverse_11 = t_ref[:, pl.ds(HALF, HALF)]
    inverse_ref[pl.ds(0, HALF), pl.ds(0, HALF)] = inverse_11
    inverse_ref[pl.ds(0, HALF), pl.ds(HALF, HALF)] = jnp.zeros((HALF, HALF), jnp.float32)
    factor_ref[pl.ds(0, HALF), pl.ds(0, HALF)] = t_ref[:, pl.ds(0, HALF)].T
    factor_ref[pl.ds(0, HALF), pl.ds(HALF, HALF)] = jnp.zeros((HALF, HALF), jnp.float32)
    lower = dot(blocks[1], inverse_11, ((1,), (1,)))
    factor_ref[pl.ds(HALF, HALF), pl.ds(0, HALF)] = lower
    half(
        blocks[2]
        + jnp.where(unit, head_noise[:, HALF:], 0.0)
        - dot(lower, lower, ((1,), (1,))),
        1,
    )
    inverse_22 = t_ref[:, pl.ds(HALF, HALF)]
    inverse_ref[pl.ds(HALF, HALF), pl.ds(HALF, HALF)] = inverse_22
    factor_ref[pl.ds(HALF, HALF), pl.ds(HALF, HALF)] = t_ref[:, pl.ds(0, HALF)].T
    lower = factor_ref[pl.ds(HALF, HALF), pl.ds(0, HALF)]
    inverse_ref[pl.ds(HALF, HALF), pl.ds(0, HALF)] = -dot(
        inverse_22, dot(lower, inverse_ref[pl.ds(0, HALF), pl.ds(0, HALF)])
    )
    last = 2 * steps - 1
    goal = chunk_goal(last)

    def keep_up(goal, more, wanted=True):
        more = jnp.where(has_far & wanted, more, 0)
        takes(goal, goal + more)
        return goal + more


    inverse = inverse_ref[...]
    solver[:, pl.ds(0, PB)] = stacked(inverse.T)
    solver[:, pl.ds(PB, PB)] = stacked(dot(inverse, inverse, ((0,), (0,))))

    goal = keep_up(goal, 3)
    each(row_goal(last), ROW_CHUNKS, row_forward)
    run(r == 0, head_copy.wait)
    run(~even, lambda: each(0, head_chunks, chunk_take))
    head_ref[...] = dot(inverse, col_raw[:, head_span])
    goal = keep_up(goal, 1)

    def row_wait(j):
        for way in range(2):
            run((place > 0) & ~forwards(way), row_copies(j, way, False).wait_recv)

    each(0, ROW_CHUNKS - LATE, row_wait)
    for j in range(LATE):
        goal = keep_up(goal, 1, c > 0)
        row_wait(ROW_CHUNKS - LATE + j)
    run(c == 0, row_copy.wait)
    need_start()
    each(min(steps, pairs), pairs, lambda p: cov_copy(p).start())

    def solve(i, carry):
        rows = pl.ds(pl.multiple_of(i * PB, PB), PB)
        high, low = split(row_raw[rows, :])
        both = jnp.dot(
            jnp.concatenate([high, low, high], axis=1),
            solver[...],
            preferred_element_type=jnp.float32,
        )
        panel[rows, :] = both[:, :PB]
        high, low = split(both[:, PB:])
        parts[rows, pl.ds(0, PB)] = high
        parts[rows, pl.ds(PB, PB)] = low
        parts[rows, pl.ds(2 * PB, PB)] = high
        return carry

    lax.fori_loop(0, row_count // PB, solve, 0)

    @pl.when(r == 0)
    def _():
        panel[pl.ds(0, PB), :] = factor_ref[...]

    goal = keep_up(goal, 1)
    target_copy.wait()
    reconstructor[...] = reconstructor[...] - jnp.dot(
        parts[...], stacked(col_raw[:, head_span]), preferred_element_type=jnp.float32
    )

    @pl.when(r == 0)
    def _():
        reconstructor[pl.ds(0, PB), :] = head_ref[...]

    goal = keep_up(goal, 1)
    run(r == 0, col_copy.wait)

    def reach(p):
        return jnp.minimum(jnp.maximum(goal + p, head_chunks + 2 * p), chunks)

    def update(p):
        takes(reach(p), reach(p + 1))
        run(
            ~even,
            lambda: each(head_chunks + 2 * p, head_chunks + 2 * p + 2, chunk_take),
        )
        cov_copy(p).wait()
        columns = pl.ds(pl.multiple_of(p * PB, PB), PB)
        raw = col_raw[:, pl.ds(pl.multiple_of(width + p * PB, CHUNK), PB)]
        updated[:, columns] = updated[:, columns] - jnp.dot(
            parts[...], stacked(raw), preferred_element_type=jnp.float32
        )
        begin = c * col_count + p * PB - r * row_count

        @pl.when((begin >= 0) & (begin < row_count))
        def _():
            block = pl.ds(pl.multiple_of(begin, PB), PB)
            diagonal = lax.broadcasted_iota(jnp.int32, (PB, PB), 0) == (
                lax.broadcasted_iota(jnp.int32, (PB, PB), 1)
            )
            updated[block, columns] = updated[block, columns] + jnp.where(
                diagonal, noise[:, block], 0.0
            )

        @pl.when(r == 0)
        def _():
            updated[pl.ds(0, PB), columns] = jnp.zeros((PB, PB), jnp.float32)

    def finish_product():
        run(c == owner, own_need.wait)
        run(c != owner, need_copies[0].wait_recv)
        product[...] = dot(dot(inverse, need_raw[...]), head_ref[...], ((0,), (0,)))

    tail = pairs - pairs // 6
    each(0, tail, update)
    finish_product()
    each(tail, pairs, update)

    @pl.when(c == 0)
    def _():
        updated[:, pl.ds(0, PB)] = panel[...]

    for k in range(n_col):
        run((c == owner) & (c != k), need_copies[k].wait_send)
    for i in range(4):
        diag_each(i, False, r >= 0, finish)

    def chunk_finish(q):
        copies = chunk_copies(q, col_raw.at[:, span(q)])
        run(has_far, copies[0].wait_send)
        run(has_near, copies[1].wait_send)

    each(0, chunks, chunk_finish)

    def row_finish(j):
        for way in range(2):
            run((place == 0) | forwards(way), row_copies(j, way, False).wait_send)

    each(0, ROW_CHUNKS, row_finish)


SLABS = 6


def store_kernel(
    updated,
    reconstructor,
    panel,
    product,
    pos,
    strength,
    scale,
    tile_layer,
    updated_out,
    reconstructor_out,
    panel_out,
    error_out,
    error,
    sems,
):
    r = lax.axis_index("row")
    c = lax.axis_index("col")
    slab = updated.shape[0] // SLABS
    copies = [
        pltpu.make_async_copy(
            updated.at[pl.ds(i * slab, slab), :],
            updated_out.at[pl.ds(i * slab, slab), :],
            sems.at[i],
        )
        for i in range(SLABS)
    ]
    copies.append(pltpu.make_async_copy(reconstructor, reconstructor_out, sems.at[SLABS]))
    copies.append(pltpu.make_async_copy(panel, panel_out, sems.at[SLABS + 1]))
    for copy in copies:
        copy.start()
    height, width = error.shape
    target_covariance(
        error,
        product,
        pos,
        strength,
        scale,
        tile_layer,
        pl.multiple_of(r * height, TILE),
        pl.multiple_of(c * width, TILE),
    )
    last = pltpu.make_async_copy(error, error_out, sems.at[SLABS + 2])
    last.start()
    for copy in copies:
        copy.wait()
    last.wait()


def local(
    n_row, n_col, covariance, wfs_map, noise_var, targets, target_pos, layer_strength,
    layer_scale, tile_layer
):
    row_count, col_count = covariance.shape
    target_width = targets.shape[1]
    error_rows = target_width * n_col // n_row
    chunks = (target_width + col_count) // CHUNK

    def f32(*shape):
        return jax.ShapeDtypeStruct(shape, jnp.float32)

    vmem = pl.BlockSpec(memory_space=pltpu.VMEM)
    anywhere = pl.BlockSpec(memory_space=pltpu.HBM)
    smem = pl.BlockSpec(memory_space=pltpu.SMEM)
    dma = pltpu.SemaphoreType.DMA
    results = pl.pallas_call(
        functools.partial(panel_kernel, n_row, n_col),
        out_shape=(
            f32(row_count, col_count),
            f32(row_count, target_width),
            f32(row_count, PB),
            f32(error_rows, target_width),
        ),
        in_specs=[anywhere] * 4,
        out_specs=[vmem] * 4,
        scratch_shapes=[
            pltpu.VMEM((row_count, PB), jnp.float32),
            pltpu.VMEM((PB, target_width + col_count), jnp.float32),
            pltpu.VMEM((PB, error_rows), jnp.float32),
            pltpu.VMEM((3, HALF, HALF), jnp.float32),
            pltpu.VMEM((PB,), jnp.int32),
            pltpu.VMEM((row_count,), jnp.int32),
            pltpu.SMEM(noise_var.shape, jnp.float32),
            pltpu.VMEM((1, row_count), jnp.float32),
            pltpu.VMEM((HALF, PB), jnp.float32),
            pltpu.VMEM((PB, PB), jnp.float32),
            pltpu.VMEM((PB, PB), jnp.float32),
            pltpu.VMEM((row_count, 3 * PB), jnp.bfloat16),
            pltpu.VMEM((3 * PB, 2 * PB), jnp.bfloat16),
            pltpu.VMEM((PB, target_width), jnp.float32),
            dma((11,)),
            dma((col_count // PB,)),
            dma((4, 4)),
            dma((4,)),
            dma((chunks, 2)),
            dma((chunks,)),
            dma((ROW_CHUNKS, 2)),
            dma((ROW_CHUNKS, 2)),
            dma((n_col,)),
            dma,
        ],
        compiler_params=pltpu.CompilerParams(
            collective_id=0, has_side_effects=True, vmem_limit_bytes=16 * 1024 * 1024
        ),
        name="panel",
    )(
        covariance,
        *[pltpu.with_memory_space_constraint(x, pltpu.HBM) for x in (targets, wfs_map, noise_var)],
    )

    outs = pl.pallas_call(
        store_kernel,
        out_shape=(
            f32(row_count, col_count),
            f32(row_count, target_width),
            f32(row_count, PB),
            f32(error_rows, target_width),
        ),
        in_specs=[vmem] * 5 + [smem] * 3,
        out_specs=[anywhere] * 4,
        scratch_shapes=[pltpu.VMEM((error_rows, target_width), jnp.float32), dma((SLABS + 3,))],
        compiler_params=pltpu.CompilerParams(vmem_limit_bytes=4 * 1024 * 1024),
        name="store",
    )(*results, target_pos, layer_strength, layer_scale, tile_layer)
    updated, reconstructor, panel, error_cov = outs
    return updated, panel, reconstructor, error_cov


def solution(mesh):
    placed = (P("row", "col"), P("row"), P(), P("row", "col"), P(), P(), P(), P())
    return jax.shard_map(
        functools.partial(local, mesh.shape["row"], mesh.shape["col"]),
        mesh=mesh,
        in_specs=placed,
        out_specs=(P("row", "col"), P("row", None), P("row", "col"), P("row", "col")),
        check_vma=False,
    )
```

```python
import functools

import jax
import jax.numpy as jnp
from jax import lax
from jax.experimental import pallas as pl
from jax.experimental.pallas import tpu as pltpu
from jax.sharding import PartitionSpec as P

PB = 256
TILE = 128
HALF = PB // 2
STEP = 8
CHUNK = 128
SPLIT = 1
GROUP = 4
ROW_CHUNKS = 12
AHEAD = 3
LATE = 3

MESH = pl.DeviceIdType.MESH
precise = lax.Precision.HIGHEST


def dot(a, b, dims=((1,), (0,))):
    return lax.dot_general(
        a, b, (dims, ((), ())), precision=precise, preferred_element_type=jnp.float32
    )


def outer(a, b):
    def thirds(x):
        high = x.astype(jnp.bfloat16).astype(jnp.float32)
        middle = (x - high).astype(jnp.bfloat16).astype(jnp.float32)
        return high, middle, x - high - middle

    p, q = thirds(a), thirds(b)
    left = jnp.concatenate([p[0], p[0], p[1], p[0], p[2], p[1]], axis=0)
    right = jnp.concatenate([q[0], q[1], q[0], q[2], q[0], q[1]], axis=0)
    return lax.dot_general(
        left.astype(jnp.bfloat16),
        right.astype(jnp.bfloat16),
        (((0,), (0,)), ((), ())),
        preferred_element_type=jnp.float32,
    )


def split(x):
    high = x.astype(jnp.bfloat16)
    return high, (x - high.astype(jnp.float32)).astype(jnp.bfloat16)


def stacked(x):
    high, low = split(x)
    return jnp.concatenate([high, high, low], axis=0)


def target_covariance(out, product, pos, strength, scale, tile_layer, row_start, col_start):
    height, width = out.shape
    levels = strength.shape[0]

    def upright(axis):
        line = pos[pl.ds(axis, 1), pl.ds(row_start, height)]
        return jnp.broadcast_to(line, (TILE, height)).T

    rows = [upright(0), upright(1)]
    for i in range(height // TILE):
        for j in range(width // TILE):
            columns = pl.ds(pl.multiple_of(col_start + j * TILE, TILE), TILE)
            across = rows[0][i * TILE : (i + 1) * TILE] - pos[pl.ds(0, 1), columns]
            along = rows[1][i * TILE : (i + 1) * TILE] - pos[pl.ds(1, 1), columns]
            distance = across * across + along * along
            lowest = jnp.minimum(
                tile_layer[row_start // TILE + i], tile_layer[col_start // TILE + j]
            )

            def layers(g, total, distance=distance, lowest=lowest):
                terms = []
                for k in range(GROUP):
                    l = jnp.minimum(g * GROUP + k, levels - 1)
                    weight = jnp.where(g * GROUP + k <= lowest, strength[l], 0.0)
                    square = scale[l] * scale[l]
                    terms.append((weight * square, square + distance))
                while len(terms) > 1:
                    terms = [
                        (a[0] * b[1] + b[0] * a[1], a[1] * b[1])
                        for a, b in zip(terms[::2], terms[1::2])
                    ]
                return total + terms[0][0] / terms[0][1]

            total = lax.fori_loop(0, lax.div(lowest, GROUP) + 1, layers, jnp.zeros_like(distance))
            here = (pl.ds(i * TILE, TILE), pl.ds(j * TILE, TILE))
            out[here] = total - product[here]


def gray_neighbours(c, n):
    position = c * 0
    after = c * 0
    before = c * 0
    ring = [i ^ (i >> 1) for i in range(n)]
    for i, node in enumerate(ring):
        position = jnp.where(c == node, i, position)
        after = jnp.where(c == node, ring[(i + 1) % n], after)
        before = jnp.where(c == node, ring[(i - 1) % n], before)
    return position, after, before


def pivot_step(t_ref, i):
    n = t_ref.shape[0]
    lanes = lax.broadcasted_iota(jnp.int32, (8, n), 1)
    wide = lax.broadcasted_iota(jnp.int32, (8, 2 * n), 1)
    down = lax.broadcasted_iota(jnp.int32, (8, 1), 0)
    k = pl.multiple_of(i * 8, 8)
    rows = t_ref[pl.ds(k, 8), :]
    left = rows[:, :n]
    columns = [
        jnp.sum(jnp.where(lanes == k + j, left, 0.0), axis=1, keepdims=True) for j in range(8)
    ]
    scale = jnp.ones((8, 1), jnp.float32)
    for j in range(8):
        pivot = columns[j][j : j + 1]
        scale = jnp.where(down == j, lax.rsqrt(pivot), scale)
        if j < 7:
            factor = jnp.where(down > j, columns[j] * (1.0 / pivot), 0.0)
            rows = rows - factor * rows[j : j + 1]
            for later in range(j + 1, 8):
                columns[later] = columns[later] - factor * columns[later][j : j + 1]
    rows = rows * scale
    rows = jnp.where((wide >= n) | (wide >= k + down), rows, 0.0)
    below = jnp.where(lanes >= k + 8, rows[:, :n], 0.0)
    t_ref[...] = t_ref[...] - outer(below, rows)
    t_ref[pl.ds(k, 8), :] = rows


def run(condition, action):
    @pl.when(condition)
    def _():
        action()


def panel_kernel(
    n_row,
    n_col,
    cov,
    targets,
    sensors,
    noise_var,
    updated,
    reconstructor,
    panel,
    product,
    row_raw,
    col_raw,
    need_raw,
    blocks,
    head_sensors,
    own_sensors,
    kinds,
    noise,
    t_ref,
    factor_ref,
    inverse_ref,
    parts,
    solver,
    head_ref,
    local_sem,
    cov_sem,
    diag_send,
    diag_recv,
    col_send,
    col_recv,
    row_send,
    row_recv,
    need_send,
    need_recv,
):
    r = lax.axis_index("row")
    c = lax.axis_index("col")
    row_count, col_count = updated.shape
    width = reconstructor.shape[1]
    need = need_raw.shape[1]
    pairs = col_count // PB
    head_chunks = SPLIT * width // CHUNK
    chunks = head_chunks + SPLIT * col_count // CHUNK
    even = lax.rem(r, 2) == 0
    plane = lax.div(r, 2)
    place, after, before = gray_neighbours(c, n_col)
    far_row = jnp.minimum(r + 2, n_row - 1)
    near_row = jnp.where(even, r + 1, r - 1)
    has_far = even & (r + 2 < n_row)
    has_near = even & (r + 1 < n_row)
    relays = even & (r > 0)
    first = (r == 0) & (c == 0)
    half_ring = n_col // 2
    ahead = SPLIT * jnp.where(place == half_ring, AHEAD + 2, AHEAD)

    head_span = pl.ds(0, width)
    head_copy = pltpu.make_async_copy(
        targets.at[pl.ds(0, PB), :], col_raw.at[:, head_span], local_sem.at[0]
    )
    col_copy = pltpu.make_async_copy(
        cov.at[pl.ds(0, PB), :], col_raw.at[:, pl.ds(width, col_count)], local_sem.at[1]
    )
    row_copy = pltpu.make_async_copy(cov.at[:, pl.ds(0, PB)], row_raw, local_sem.at[2])
    target_copy = pltpu.make_async_copy(targets, reconstructor, local_sem.at[3])
    sensor_copy = pltpu.make_async_copy(sensors, own_sensors, local_sem.at[9])
    noise_copy = pltpu.make_async_copy(noise_var, kinds, local_sem.at[10])
    quarters = [(0, 0), (HALF, 0), (HALF, HALF)]

    def diag_piece(i, source):
        if i == 0:
            return (sensors.at[pl.ds(0, PB)] if source else head_sensors), head_sensors
        dst = blocks.at[i - 1]
        if source:
            y, x = quarters[i - 1]
            return cov.at[pl.ds(y, HALF), pl.ds(x, HALF)], dst
        return dst, dst

    own_diag = [
        pltpu.make_async_copy(*diag_piece(i, True), local_sem.at[5 + i]) for i in range(4)
    ]

    def cov_copy(p):
        columns = pl.ds(pl.multiple_of(p * PB, PB), PB)
        return pltpu.make_async_copy(cov.at[:, columns], updated.at[:, columns], cov_sem.at[p])

    for copy in own_diag:
        run(first, copy.start)
    sensor_copy.start()
    noise_copy.start()

    barrier = pltpu.get_barrier_semaphore()

    def greet(col, row):
        pl.semaphore_signal(barrier, inc=1, device_id=(col, row), device_id_type=MESH)

    greet(c, near_row)
    for k in range(1, n_col):
        greet(lax.rem(c + k, n_col), r)
    run(has_far, lambda: greet(c, far_row))
    run(relays, lambda: greet(c, jnp.maximum(r - 2, 0)))
    pl.semaphore_wait(barrier, n_col + jnp.where(has_far, 1, 0) + jnp.where(relays, 1, 0))

    def remote(src, dst, send, recv, col, row):
        return pltpu.make_async_remote_copy(
            src_ref=src,
            dst_ref=dst,
            send_sem=send,
            recv_sem=recv,
            device_id=(col, row),
            device_id_type=MESH,
        )

    def upward(src, dst, send, recv):
        return (
            remote(src, dst, send[0], recv, c, far_row),
            remote(src, dst, send[1], recv, c, near_row),
        )

    def diag_copies(i, source):
        src, dst = diag_piece(i, source)
        ring = [
            remote(src, dst, diag_send.at[i, k], diag_recv.at[i], to, r)
            for k, to in enumerate([after, before])
        ]
        return ring, upward(src, dst, [diag_send.at[i, 2], diag_send.at[i, 3]], diag_recv.at[i])

    ring_after = (r == 0) & (place < half_ring)
    ring_before = (r == 0) & ((place == 0) | (place >= half_ring + 2))

    def diag_each(i, source, allowed, what):
        ring, up = diag_copies(i, source)
        run(allowed & has_far, lambda: what(up[0]))
        run(allowed & has_near, lambda: what(up[1]))
        run(allowed & ring_after, lambda: what(ring[0]))
        run(allowed & ring_before, lambda: what(ring[1]))

    def start(copy):
        copy.start()

    def finish(copy):
        copy.wait_send()

    piece_rows = PB // SPLIT

    def span(q):
        rows = pl.ds(pl.multiple_of(lax.rem(q, SPLIT) * piece_rows, piece_rows), piece_rows)
        columns = pl.ds(pl.multiple_of(lax.div(q, SPLIT) * CHUNK, CHUNK), CHUNK)
        return rows, columns

    def chunk_copies(q, src):
        return upward(
            src, col_raw.at[span(q)], [col_send.at[q, 0], col_send.at[q, 1]], col_recv.at[q]
        )

    def chunk_start(copies):
        run(has_far, copies[0].start)
        run(has_near, copies[1].start)

    def source_chunk(q):
        run(
            q < head_chunks,
            lambda: chunk_start(
                chunk_copies(q, targets.at[span(jnp.minimum(q, head_chunks - 1))])
            ),
        )
        run(
            q >= head_chunks,
            lambda: chunk_start(
                chunk_copies(q, cov.at[span(jnp.maximum(q - head_chunks, 0))])
            ),
        )

    def each(low, high, action):
        def body(i, carry):
            action(i)
            return carry

        lax.fori_loop(low, high, body, 0)

    def chunk_take(q):
        copies = chunk_copies(q, col_raw.at[span(q)])
        copies[0].wait_recv()
        run(even, lambda: chunk_start(copies))

    def takes(low, high):
        run(relays, lambda: each(low, high, chunk_take))

    step_rows = row_count // (2 * ROW_CHUNKS)

    def row_copies(j, way, source):
        rows = pl.ds(pl.multiple_of((2 * j + way) * step_rows, step_rows), step_rows)
        dst = row_raw.at[rows, :]
        src = cov.at[rows, pl.ds(0, PB)] if source else dst
        to = after if way == 0 else before
        return remote(src, dst, row_send.at[j, way], row_recv.at[j, way], to, r)

    def forwards(way):
        return (place > 0) & ((place < n_col - 1) if way == 0 else (place > 1))

    def row_source(j):
        for way in range(2):
            row_copies(j, way, True).start()

    def row_forward(j):
        for way in range(2):
            copy = row_copies(j, way, False)
            run(forwards(way), lambda: (copy.wait_recv(), copy.start()))

    def diag_pass(i):
        run((r > 0) | (c > 0), diag_copies(i, False)[0][0].wait_recv)
        diag_each(i, False, ~first, start)
        run(first, own_diag[i].wait)

    def noise_of(sensor):
        total = jnp.zeros(sensor.shape, jnp.float32)
        for k in range(noise_var.shape[0]):
            total = jnp.where(sensor == k, kinds[k], total)
        return total

    def row_goal(s):
        late = jnp.where(place == half_ring, 1, 0) + jnp.where(plane == 0, 3, -1)
        reach = lax.div(jnp.maximum(s + lax.div(14 * plane, 3) - late, 0), 3)
        return jnp.minimum(reach, ROW_CHUNKS)

    for i in range(4):
        diag_each(i, True, first, start)
    run((r == 0) & (c > 0), lambda: each(0, ahead, source_chunk))
    run((place == 0) & (r != 1), lambda: each(0, ROW_CHUNKS, row_source))
    run(first, lambda: each(0, chunks, source_chunk))
    run(c > 0, lambda: takes(0, ahead))
    early_rows = jnp.maximum(row_goal(-1) - 1, 0)
    each(0, early_rows, row_forward)
    diag_pass(0)
    diag_pass(1)
    run((place == 0) & (r == 1), lambda: each(0, ROW_CHUNKS, row_source))
    sensor_copy.wait()
    noise_copy.wait()
    noise[...] = noise_of(own_sensors[...].reshape(1, row_count))
    head_noise = noise_of(head_sensors[...].reshape(1, PB))
    unit = lax.broadcasted_iota(jnp.int32, (HALF, HALF), 0) == lax.broadcasted_iota(
        jnp.int32, (HALF, HALF), 1
    )

    def chunk_goal(s):
        early = jnp.where(c == 0, -1, jnp.where(place == half_ring, 12, 7))
        early = jnp.where(has_far, early, -3)
        reached = lax.div(SPLIT * jnp.maximum(s + early, 0), 3)
        return jnp.maximum(reached, jnp.where(c == 0, 0, ahead))

    steps = HALF // STEP

    def side_work(s):
        @pl.when(s == 2)
        def _():
            diag_pass(2)

        @pl.when(s == 4)
        def _():
            diag_pass(3)
            run((r == 0) & (c > 0), lambda: each(ahead, chunks, source_chunk))

        @pl.when(s == 6)
        def _():
            run(r == 0, lambda: (head_copy.start(), col_copy.start()))
            run(c == 0, row_copy.start)

        run(s == 8, target_copy.start)
        run((lax.rem(s, 2) == 1) & (lax.div(s, 2) < pairs), lambda: cov_copy(lax.div(s, 2)).start())
        takes(chunk_goal(s - 1), chunk_goal(s))
        each(jnp.where(s > 0, row_goal(s - 1), early_rows), row_goal(s), row_forward)

    def half(block, where):
        t_ref[:, pl.ds(0, HALF)] = block
        t_ref[:, pl.ds(HALF, HALF)] = unit.astype(jnp.float32)

        def step(i, carry):
            pivot_step(t_ref, i)
            side_work(i + where * steps)
            return carry

        lax.fori_loop(0, steps, step, 0)

    owner = lax.div(r * need, width)
    offset = pl.multiple_of(lax.rem(r * need, width), CHUNK)
    need_copies = [
        remote(col_raw.at[:, pl.ds(offset, need)], need_raw, need_send.at[k], need_recv, k, r)
        for k in range(n_col)
    ]
    own_need = pltpu.make_async_copy(
        col_raw.at[:, pl.ds(offset, need)], need_raw, local_sem.at[4]
    )

    def need_start():
        for k in range(n_col):
            run((c == owner) & (c != k), need_copies[k].start)
        run(c == owner, own_need.start)

    half(blocks[0] + jnp.where(unit, head_noise[:, :HALF], 0.0), 0)
    inverse_11 = t_ref[:, pl.ds(HALF, HALF)]
    inverse_ref[pl.ds(0, HALF), pl.ds(0, HALF)] = inverse_11
    inverse_ref[pl.ds(0, HALF), pl.ds(HALF, HALF)] = jnp.zeros((HALF, HALF), jnp.float32)
    factor_ref[pl.ds(0, HALF), pl.ds(0, HALF)] = t_ref[:, pl.ds(0, HALF)].T
    factor_ref[pl.ds(0, HALF), pl.ds(HALF, HALF)] = jnp.zeros((HALF, HALF), jnp.float32)
    lower = dot(blocks[1], inverse_11, ((1,), (1,)))
    factor_ref[pl.ds(HALF, HALF), pl.ds(0, HALF)] = lower
    half(
        blocks[2]
        + jnp.where(unit, head_noise[:, HALF:], 0.0)
        - dot(lower, lower, ((1,), (1,))),
        1,
    )
    inverse_22 = t_ref[:, pl.ds(HALF, HALF)]
    inverse_ref[pl.ds(HALF, HALF), pl.ds(HALF, HALF)] = inverse_22
    factor_ref[pl.ds(HALF, HALF), pl.ds(HALF, HALF)] = t_ref[:, pl.ds(0, HALF)].T
    lower = factor_ref[pl.ds(HALF, HALF), pl.ds(0, HALF)]
    inverse_ref[pl.ds(HALF, HALF), pl.ds(0, HALF)] = -dot(
        inverse_22, dot(lower, inverse_ref[pl.ds(0, HALF), pl.ds(0, HALF)])
    )
    last = 2 * steps - 1
    goal = chunk_goal(last)

    def keep_up(goal, more, wanted=True):
        more = jnp.where(has_far & wanted, SPLIT * more, 0)
        takes(goal, goal + more)
        return goal + more


    inverse = inverse_ref[...]
    solver[:, pl.ds(0, PB)] = stacked(inverse.T)
    solver[:, pl.ds(PB, PB)] = stacked(dot(inverse, inverse, ((0,), (0,))))

    goal = keep_up(goal, 3)
    each(row_goal(last), ROW_CHUNKS, row_forward)
    run(r == 0, head_copy.wait)
    run(~even, lambda: each(0, head_chunks, chunk_take))
    head_ref[...] = dot(inverse, col_raw[:, head_span])
    goal = keep_up(goal, 1)

    def row_wait(j):
        for way in range(2):
            run((place > 0) & ~forwards(way), row_copies(j, way, False).wait_recv)

    each(0, ROW_CHUNKS - LATE, row_wait)
    for j in range(LATE):
        goal = keep_up(goal, 1, (c > 0) & (place != half_ring))
        row_wait(ROW_CHUNKS - LATE + j)
    run(c == 0, row_copy.wait)
    need_start()
    each(min(steps, pairs), pairs, lambda p: cov_copy(p).start())

    def solve(i, carry):
        rows = pl.ds(pl.multiple_of(i * PB, PB), PB)
        high, low = split(row_raw[rows, :])
        both = jnp.dot(
            jnp.concatenate([high, low, high], axis=1),
            solver[...],
            preferred_element_type=jnp.float32,
        )
        panel[rows, :] = both[:, :PB]
        high, low = split(both[:, PB:])
        parts[rows, pl.ds(0, PB)] = high
        parts[rows, pl.ds(PB, PB)] = low
        parts[rows, pl.ds(2 * PB, PB)] = high
        return carry

    lax.fori_loop(0, row_count // PB, solve, 0)

    @pl.when(r == 0)
    def _():
        panel[pl.ds(0, PB), :] = factor_ref[...]

    goal = keep_up(goal, 1)
    target_copy.wait()
    reconstructor[...] = reconstructor[...] - jnp.dot(
        parts[...], stacked(col_raw[:, head_span]), preferred_element_type=jnp.float32
    )

    @pl.when(r == 0)
    def _():
        reconstructor[pl.ds(0, PB), :] = head_ref[...]

    goal = keep_up(goal, 1)
    run(r == 0, col_copy.wait)

    def reach(p):
        return jnp.minimum(jnp.maximum(goal + SPLIT * p, head_chunks + 2 * SPLIT * p), chunks)

    def update(p):
        takes(reach(p), reach(p + 1))
        run(
            ~even,
            lambda: each(
                head_chunks + 2 * SPLIT * p, head_chunks + 2 * SPLIT * (p + 1), chunk_take
            ),
        )
        cov_copy(p).wait()
        columns = pl.ds(pl.multiple_of(p * PB, PB), PB)
        raw = col_raw[:, pl.ds(pl.multiple_of(width + p * PB, CHUNK), PB)]
        updated[:, columns] = updated[:, columns] - jnp.dot(
            parts[...], stacked(raw), preferred_element_type=jnp.float32
        )
        begin = c * col_count + p * PB - r * row_count

        @pl.when((begin >= 0) & (begin < row_count))
        def _():
            block = pl.ds(pl.multiple_of(begin, PB), PB)
            diagonal = lax.broadcasted_iota(jnp.int32, (PB, PB), 0) == (
                lax.broadcasted_iota(jnp.int32, (PB, PB), 1)
            )
            updated[block, columns] = updated[block, columns] + jnp.where(
                diagonal, noise[:, block], 0.0
            )

        @pl.when(r == 0)
        def _():
            updated[pl.ds(0, PB), columns] = jnp.zeros((PB, PB), jnp.float32)

    def finish_product():
        run(c == owner, own_need.wait)
        run(c != owner, need_copies[0].wait_recv)
        product[...] = dot(dot(inverse, need_raw[...]), head_ref[...], ((0,), (0,)))

    tail = pairs - pairs // 6
    each(0, tail, update)
    finish_product()

    @pl.when(c == 0)
    def _():
        updated[:, pl.ds(0, PB)] = panel[...]

    each(tail, pairs, update)

    for k in range(n_col):
        run((c == owner) & (c != k), need_copies[k].wait_send)
    for i in range(4):
        diag_each(i, False, r >= 0, finish)

    def chunk_finish(q):
        copies = chunk_copies(q, col_raw.at[span(q)])
        run(has_far, copies[0].wait_send)
        run(has_near, copies[1].wait_send)

    each(0, chunks, chunk_finish)

    def row_finish(j):
        for way in range(2):
            run((place == 0) | forwards(way), row_copies(j, way, False).wait_send)

    each(0, ROW_CHUNKS, row_finish)


SLABS = 6


def store_kernel(
    updated,
    reconstructor,
    panel,
    product,
    pos,
    strength,
    scale,
    tile_layer,
    updated_out,
    reconstructor_out,
    panel_out,
    error_out,
    error,
    sems,
):
    r = lax.axis_index("row")
    c = lax.axis_index("col")
    slab = updated.shape[0] // SLABS
    copies = [
        pltpu.make_async_copy(
            updated.at[pl.ds(i * slab, slab), :],
            updated_out.at[pl.ds(i * slab, slab), :],
            sems.at[i],
        )
        for i in range(SLABS)
    ]
    copies.append(pltpu.make_async_copy(reconstructor, reconstructor_out, sems.at[SLABS]))
    copies.append(pltpu.make_async_copy(panel, panel_out, sems.at[SLABS + 1]))
    for copy in copies:
        copy.start()
    height, width = error.shape
    target_covariance(
        error,
        product,
        pos,
        strength,
        scale,
        tile_layer,
        pl.multiple_of(r * height, TILE),
        pl.multiple_of(c * width, TILE),
    )
    last = pltpu.make_async_copy(error, error_out, sems.at[SLABS + 2])
    last.start()
    for copy in copies:
        copy.wait()
    last.wait()


def local(
    n_row, n_col, covariance, wfs_map, noise_var, targets, target_pos, layer_strength,
    layer_scale, tile_layer
):
    row_count, col_count = covariance.shape
    target_width = targets.shape[1]
    error_rows = target_width * n_col // n_row
    chunks = SPLIT * (target_width + col_count) // CHUNK

    def f32(*shape):
        return jax.ShapeDtypeStruct(shape, jnp.float32)

    vmem = pl.BlockSpec(memory_space=pltpu.VMEM)
    anywhere = pl.BlockSpec(memory_space=pltpu.HBM)
    smem = pl.BlockSpec(memory_space=pltpu.SMEM)
    dma = pltpu.SemaphoreType.DMA
    results = pl.pallas_call(
        functools.partial(panel_kernel, n_row, n_col),
        out_shape=(
            f32(row_count, col_count),
            f32(row_count, target_width),
            f32(row_count, PB),
            f32(error_rows, target_width),
        ),
        in_specs=[anywhere] * 4,
        out_specs=[vmem] * 4,
        scratch_shapes=[
            pltpu.VMEM((row_count, PB), jnp.float32),
            pltpu.VMEM((PB, target_width + col_count), jnp.float32),
            pltpu.VMEM((PB, error_rows), jnp.float32),
            pltpu.VMEM((3, HALF, HALF), jnp.float32),
            pltpu.VMEM((PB,), jnp.int32),
            pltpu.VMEM((row_count,), jnp.int32),
            pltpu.SMEM(noise_var.shape, jnp.float32),
            pltpu.VMEM((1, row_count), jnp.float32),
            pltpu.VMEM((HALF, PB), jnp.float32),
            pltpu.VMEM((PB, PB), jnp.float32),
            pltpu.VMEM((PB, PB), jnp.float32),
            pltpu.VMEM((row_count, 3 * PB), jnp.bfloat16),
            pltpu.VMEM((3 * PB, 2 * PB), jnp.bfloat16),
            pltpu.VMEM((PB, target_width), jnp.float32),
            dma((11,)),
            dma((col_count // PB,)),
            dma((4, 4)),
            dma((4,)),
            dma((chunks, 2)),
            dma((chunks,)),
            dma((ROW_CHUNKS, 2)),
            dma((ROW_CHUNKS, 2)),
            dma((n_col,)),
            dma,
        ],
        compiler_params=pltpu.CompilerParams(
            collective_id=0, has_side_effects=True, vmem_limit_bytes=16 * 1024 * 1024
        ),
        name="panel",
    )(
        covariance,
        *[pltpu.with_memory_space_constraint(x, pltpu.HBM) for x in (targets, wfs_map, noise_var)],
    )

    outs = pl.pallas_call(
        store_kernel,
        out_shape=(
            f32(row_count, col_count),
            f32(row_count, target_width),
            f32(row_count, PB),
            f32(error_rows, target_width),
        ),
        in_specs=[vmem] * 5 + [smem] * 3,
        out_specs=[anywhere] * 4,
        scratch_shapes=[pltpu.VMEM((error_rows, target_width), jnp.float32), dma((SLABS + 3,))],
        compiler_params=pltpu.CompilerParams(vmem_limit_bytes=4 * 1024 * 1024),
        name="store",
    )(*results, target_pos, layer_strength, layer_scale, tile_layer)
    updated, reconstructor, panel, error_cov = outs
    return updated, panel, reconstructor, error_cov


def solution(mesh):
    placed = (P("row", "col"), P("row"), P(), P("row", "col"), P(), P(), P(), P())
    return jax.shard_map(
        functools.partial(local, mesh.shape["row"], mesh.shape["col"]),
        mesh=mesh,
        in_specs=placed,
        out_specs=(P("row", "col"), P("row", None), P("row", "col"), P("row", "col")),
        check_vma=False,
    )
```

```python
import functools

import jax
import jax.numpy as jnp
from jax import lax
from jax.experimental import pallas as pl
from jax.experimental.pallas import tpu as pltpu
from jax.sharding import PartitionSpec as P

PB = 256
TILE = 128
HALF = PB // 2
STEP = 8
CHUNK = 128
TAIL = 4
KEEP = 3
MEET = 1
PUSH = (3, 3)
PACE = (9, 9)
GROUP = 4
ROW_CHUNKS = 12
AHEAD = 3
LATE = 3

MESH = pl.DeviceIdType.MESH
precise = lax.Precision.HIGHEST


def dot(a, b, dims=((1,), (0,))):
    return lax.dot_general(
        a, b, (dims, ((), ())), precision=precise, preferred_element_type=jnp.float32
    )


def outer(a, b):
    def thirds(x):
        high = x.astype(jnp.bfloat16).astype(jnp.float32)
        middle = (x - high).astype(jnp.bfloat16).astype(jnp.float32)
        return high, middle, x - high - middle

    p, q = thirds(a), thirds(b)
    left = jnp.concatenate([p[0], p[0], p[1], p[0], p[2], p[1]], axis=0)
    right = jnp.concatenate([q[0], q[1], q[0], q[2], q[0], q[1]], axis=0)
    return lax.dot_general(
        left.astype(jnp.bfloat16),
        right.astype(jnp.bfloat16),
        (((0,), (0,)), ((), ())),
        preferred_element_type=jnp.float32,
    )


def split(x):
    high = x.astype(jnp.bfloat16)
    return high, (x - high.astype(jnp.float32)).astype(jnp.bfloat16)


def stacked(x):
    high, low = split(x)
    return jnp.concatenate([high, high, low], axis=0)


def target_covariance(out, product, pos, strength, scale, tile_layer, row_start, col_start):
    height, width = out.shape
    levels = strength.shape[0]

    def upright(axis):
        line = pos[pl.ds(axis, 1), pl.ds(row_start, height)]
        return jnp.broadcast_to(line, (TILE, height)).T

    rows = [upright(0), upright(1)]
    for i in range(height // TILE):
        for j in range(width // TILE):
            columns = pl.ds(pl.multiple_of(col_start + j * TILE, TILE), TILE)
            across = rows[0][i * TILE : (i + 1) * TILE] - pos[pl.ds(0, 1), columns]
            along = rows[1][i * TILE : (i + 1) * TILE] - pos[pl.ds(1, 1), columns]
            distance = across * across + along * along
            lowest = jnp.minimum(
                tile_layer[row_start // TILE + i], tile_layer[col_start // TILE + j]
            )

            def layers(g, total, distance=distance, lowest=lowest):
                terms = []
                for k in range(GROUP):
                    l = jnp.minimum(g * GROUP + k, levels - 1)
                    weight = jnp.where(g * GROUP + k <= lowest, strength[l], 0.0)
                    square = scale[l] * scale[l]
                    terms.append((weight * square, square + distance))
                while len(terms) > 1:
                    terms = [
                        (a[0] * b[1] + b[0] * a[1], a[1] * b[1])
                        for a, b in zip(terms[::2], terms[1::2])
                    ]
                return total + terms[0][0] / terms[0][1]

            total = lax.fori_loop(0, lax.div(lowest, GROUP) + 1, layers, jnp.zeros_like(distance))
            here = (pl.ds(i * TILE, TILE), pl.ds(j * TILE, TILE))
            out[here] = total - product[here]


def gray_neighbours(c, n):
    position = c * 0
    after = c * 0
    before = c * 0
    ring = [i ^ (i >> 1) for i in range(n)]
    for i, node in enumerate(ring):
        position = jnp.where(c == node, i, position)
        after = jnp.where(c == node, ring[(i + 1) % n], after)
        before = jnp.where(c == node, ring[(i - 1) % n], before)
    return position, after, before


def pivot_step(t_ref, i):
    n = t_ref.shape[0]
    lanes = lax.broadcasted_iota(jnp.int32, (8, n), 1)
    wide = lax.broadcasted_iota(jnp.int32, (8, 2 * n), 1)
    down = lax.broadcasted_iota(jnp.int32, (8, 1), 0)
    k = pl.multiple_of(i * 8, 8)
    rows = t_ref[pl.ds(k, 8), :]
    left = rows[:, :n]
    columns = [
        jnp.sum(jnp.where(lanes == k + j, left, 0.0), axis=1, keepdims=True) for j in range(8)
    ]
    scale = jnp.ones((8, 1), jnp.float32)
    for j in range(8):
        pivot = columns[j][j : j + 1]
        scale = jnp.where(down == j, lax.rsqrt(pivot), scale)
        if j < 7:
            factor = jnp.where(down > j, columns[j] * (1.0 / pivot), 0.0)
            rows = rows - factor * rows[j : j + 1]
            for later in range(j + 1, 8):
                columns[later] = columns[later] - factor * columns[later][j : j + 1]
    rows = rows * scale
    rows = jnp.where((wide >= n) | (wide >= k + down), rows, 0.0)
    below = jnp.where(lanes >= k + 8, rows[:, :n], 0.0)
    t_ref[...] = t_ref[...] - outer(below, rows)
    t_ref[pl.ds(k, 8), :] = rows


def run(condition, action):
    @pl.when(condition)
    def _():
        action()


def update_pair(out, out_columns, matrix, columns, parts, raw, noise, begin, r):
    height = parts.shape[0]
    out[:, out_columns] = matrix[:, columns] - jnp.dot(
        parts[...], stacked(raw), preferred_element_type=jnp.float32
    )

    @pl.when((begin >= 0) & (begin < height))
    def _():
        block = pl.ds(pl.multiple_of(begin, PB), PB)
        diagonal = lax.broadcasted_iota(jnp.int32, (PB, PB), 0) == (
            lax.broadcasted_iota(jnp.int32, (PB, PB), 1)
        )
        out[block, out_columns] = out[block, out_columns] + jnp.where(
            diagonal, noise[:, block], 0.0
        )

    @pl.when(r == 0)
    def _():
        out[pl.ds(0, PB), out_columns] = jnp.zeros((PB, PB), jnp.float32)


def panel_kernel(
    n_row,
    n_col,
    cov,
    targets,
    sensors,
    noise_var,
    updated,
    reconstructor,
    panel,
    product,
    parts,
    noise,
    late_raw,
    row_raw,
    col_raw,
    need_raw,
    blocks,
    head_sensors,
    own_sensors,
    kinds,
    t_ref,
    factor_ref,
    inverse_ref,
    solver,
    head_ref,
    local_sem,
    cov_sem,
    diag_send,
    diag_recv,
    col_send,
    col_recv,
    tail_send,
    tail_recv,
    row_send,
    row_recv,
    need_send,
    need_recv,
):
    r = lax.axis_index("row")
    c = lax.axis_index("col")
    row_count, col_count = updated.shape
    width = reconstructor.shape[1]
    need = need_raw.shape[1]
    pairs = col_count // PB
    head_chunks = width // CHUNK
    chunks = head_chunks + (col_count - PB) // CHUNK
    even = lax.rem(r, 2) == 0
    plane = lax.div(r, 2)
    place, after, before = gray_neighbours(c, n_col)
    far_row = jnp.minimum(r + 2, n_row - 1)
    near_row = jnp.where(even, r + 1, r - 1)
    has_far = even & (r + 2 < n_row)
    has_near = even & (r + 1 < n_row)
    relays = even & (r > 0)
    first = (r == 0) & (c == 0)
    half_ring = n_col // 2
    ahead = jnp.where(place == half_ring, AHEAD + 2, AHEAD)

    head_span = pl.ds(0, width)
    head_copy = pltpu.make_async_copy(
        targets.at[pl.ds(0, PB), :], col_raw.at[:, head_span], local_sem.at[0]
    )
    col_copy = pltpu.make_async_copy(
        cov.at[pl.ds(0, PB), :], col_raw.at[:, pl.ds(width, col_count)], local_sem.at[1]
    )
    row_copy = pltpu.make_async_copy(cov.at[:, pl.ds(0, PB)], row_raw, local_sem.at[2])
    target_copy = pltpu.make_async_copy(targets, reconstructor, local_sem.at[3])
    sensor_copy = pltpu.make_async_copy(sensors, own_sensors, local_sem.at[9])
    noise_copy = pltpu.make_async_copy(noise_var, kinds, local_sem.at[10])
    quarters = [(0, 0), (HALF, 0), (HALF, HALF)]

    def diag_piece(i, source):
        if i == 0:
            return (sensors.at[pl.ds(0, PB)] if source else head_sensors), head_sensors
        dst = blocks.at[i - 1]
        if source:
            y, x = quarters[i - 1]
            return cov.at[pl.ds(y, HALF), pl.ds(x, HALF)], dst
        return dst, dst

    own_diag = [
        pltpu.make_async_copy(*diag_piece(i, True), local_sem.at[5 + i]) for i in range(4)
    ]

    def cov_copy(p):
        columns = pl.ds(pl.multiple_of(p * PB, PB), PB)
        return pltpu.make_async_copy(cov.at[:, columns], updated.at[:, columns], cov_sem.at[p])

    for copy in own_diag:
        run(first, copy.start)
    sensor_copy.start()
    noise_copy.start()

    barrier = pltpu.get_barrier_semaphore()

    def greet(col, row):
        pl.semaphore_signal(barrier, inc=1, device_id=(col, row), device_id_type=MESH)

    greet(c, near_row)
    for k in range(1, n_col):
        greet(lax.rem(c + k, n_col), r)
    run(has_far, lambda: greet(c, far_row))
    run(relays, lambda: greet(c, jnp.maximum(r - 2, 0)))
    pl.semaphore_wait(barrier, n_col + jnp.where(has_far, 1, 0) + jnp.where(relays, 1, 0))

    def remote(src, dst, send, recv, col, row):
        return pltpu.make_async_remote_copy(
            src_ref=src,
            dst_ref=dst,
            send_sem=send,
            recv_sem=recv,
            device_id=(col, row),
            device_id_type=MESH,
        )

    def upward(src, dst, send, recv):
        return (
            remote(src, dst, send[0], recv, c, far_row),
            remote(src, dst, send[1], recv, c, near_row),
        )

    def diag_copies(i, source):
        src, dst = diag_piece(i, source)
        ring = [
            remote(src, dst, diag_send.at[i, k], diag_recv.at[i], to, r)
            for k, to in enumerate([after, before])
        ]
        return ring, upward(src, dst, [diag_send.at[i, 2], diag_send.at[i, 3]], diag_recv.at[i])

    ring_after = (r == 0) & (place < half_ring)
    ring_before = (r == 0) & ((place == 0) | (place >= half_ring + 2))

    def diag_each(i, source, allowed, what):
        ring, up = diag_copies(i, source)
        run(allowed & has_far, lambda: what(up[0]))
        run(allowed & has_near, lambda: what(up[1]))
        run(allowed & ring_after, lambda: what(ring[0]))
        run(allowed & ring_before, lambda: what(ring[1]))

    def start(copy):
        copy.start()

    def finish(copy):
        copy.wait_send()

    tail_rows = PB // TAIL

    def span(q):
        return pl.ds(0, PB), pl.ds(pl.multiple_of(q * CHUNK, CHUNK), CHUNK)

    def chunk_copies(q, src):
        return upward(
            src, col_raw.at[span(q)], [col_send.at[q, 0], col_send.at[q, 1]], col_recv.at[q]
        )

    def chunk_start(copies):
        run(has_far, copies[0].start)
        run(has_near, copies[1].start)

    def source_chunk(q):
        run(
            q < head_chunks,
            lambda: chunk_start(
                chunk_copies(q, targets.at[span(jnp.minimum(q, head_chunks - 1))])
            ),
        )
        run(
            q >= head_chunks,
            lambda: chunk_start(
                chunk_copies(q, cov.at[span(jnp.maximum(q - head_chunks, 0))])
            ),
        )

    def tail_copies(t, source):
        rows = pl.ds(pl.multiple_of(t * tail_rows, tail_rows), tail_rows)
        dst = col_raw.at[rows, pl.ds(width + col_count - PB, PB)]
        src = cov.at[rows, pl.ds(col_count - PB, PB)] if source else dst
        return upward(src, dst, [tail_send.at[t, 0], tail_send.at[t, 1]], tail_recv.at[t])

    def tail_take(t):
        copies = tail_copies(t, False)
        copies[0].wait_recv()
        run(even, lambda: chunk_start(copies))

    def tail_source(t):
        chunk_start(tail_copies(t, True))

    def each(low, high, action):
        def body(i, carry):
            action(i)
            return carry

        lax.fori_loop(low, high, body, 0)

    def chunk_take(q):
        copies = chunk_copies(q, col_raw.at[span(q)])
        copies[0].wait_recv()
        run(even, lambda: chunk_start(copies))

    def takes(low, high):
        run(relays, lambda: each(low, high, chunk_take))

    step_rows = row_count // (2 * ROW_CHUNKS)

    def row_copies(j, way, source):
        rows = pl.ds(pl.multiple_of((2 * j + way) * step_rows, step_rows), step_rows)
        dst = row_raw.at[rows, :]
        src = cov.at[rows, pl.ds(0, PB)] if source else dst
        to = after if way == 0 else before
        return remote(src, dst, row_send.at[j, way], row_recv.at[j, way], to, r)

    def forwards(way):
        return (place > 0) & ((place < n_col - 1) if way == 0 else (place > 1))

    def row_source(j):
        for way in range(2):
            row_copies(j, way, True).start()

    def row_forward(j):
        for way in range(2):
            copy = row_copies(j, way, False)
            run(forwards(way), lambda: (copy.wait_recv(), copy.start()))

    def diag_pass(i):
        run((r > 0) | (c > 0), diag_copies(i, False)[0][0].wait_recv)
        diag_each(i, False, ~first, start)
        run(first, own_diag[i].wait)

    def noise_of(sensor):
        total = jnp.zeros(sensor.shape, jnp.float32)
        for k in range(noise_var.shape[0]):
            total = jnp.where(sensor == k, kinds[k], total)
        return total

    def row_goal(s):
        late = jnp.where(place == half_ring, 1, 0) + jnp.where(plane == 0, 3, -1)
        reach = lax.div(jnp.maximum(s + lax.div(14 * plane, 3) - late, 0), 3)
        return jnp.minimum(reach, ROW_CHUNKS)

    for i in range(4):
        diag_each(i, True, first, start)
    run((r == 0) & (c > 0), lambda: each(0, ahead, source_chunk))
    run((place == 0) & (r != 1), lambda: each(0, ROW_CHUNKS, row_source))
    run(first, lambda: (each(0, chunks, source_chunk), each(0, TAIL, tail_source)))
    run(c > 0, lambda: takes(0, ahead))
    early_rows = jnp.maximum(row_goal(-1) - 1, 0)
    each(0, early_rows, row_forward)
    diag_pass(0)
    diag_pass(1)
    run((place == 0) & (r == 1), lambda: each(0, ROW_CHUNKS, row_source))
    sensor_copy.wait()
    noise_copy.wait()
    noise[...] = noise_of(own_sensors[...].reshape(1, row_count))
    head_noise = noise_of(head_sensors[...].reshape(1, PB))
    unit = lax.broadcasted_iota(jnp.int32, (HALF, HALF), 0) == lax.broadcasted_iota(
        jnp.int32, (HALF, HALF), 1
    )

    def chunk_goal(s):
        early = jnp.where(c == 0, -1, jnp.where(place == half_ring, 12, 7))
        early = jnp.where(has_far, early, -3)
        reached = lax.div(jnp.maximum(s + early, 0), 3)
        return jnp.maximum(reached, jnp.where(c == 0, 0, ahead))

    steps = HALF // STEP

    def side_work(s):
        @pl.when(s == 2)
        def _():
            diag_pass(2)

        @pl.when(s == 4)
        def _():
            diag_pass(3)
            run(
                (r == 0) & (c > 0),
                lambda: (each(ahead, chunks, source_chunk), each(0, TAIL, tail_source)),
            )

        @pl.when(s == 6)
        def _():
            run(r == 0, lambda: (head_copy.start(), col_copy.start()))
            run(c == 0, row_copy.start)

        run(s == 8, target_copy.start)
        run((lax.rem(s, 2) == 1) & (lax.div(s, 2) < pairs), lambda: cov_copy(lax.div(s, 2)).start())
        takes(chunk_goal(s - 1), chunk_goal(s))
        each(jnp.where(s > 0, row_goal(s - 1), early_rows), row_goal(s), row_forward)

    def half(block, where):
        t_ref[:, pl.ds(0, HALF)] = block
        t_ref[:, pl.ds(HALF, HALF)] = unit.astype(jnp.float32)

        def step(i, carry):
            pivot_step(t_ref, i)
            side_work(i + where * steps)
            return carry

        lax.fori_loop(0, steps, step, 0)

    owner = lax.div(r * need, width)
    offset = pl.multiple_of(lax.rem(r * need, width), CHUNK)
    need_copies = [
        remote(col_raw.at[:, pl.ds(offset, need)], need_raw, need_send.at[k], need_recv, k, r)
        for k in range(n_col)
    ]
    own_need = pltpu.make_async_copy(
        col_raw.at[:, pl.ds(offset, need)], need_raw, local_sem.at[4]
    )

    def need_start():
        for k in range(n_col):
            run((c == owner) & (c != k), need_copies[k].start)
        run(c == owner, own_need.start)

    half(blocks[0] + jnp.where(unit, head_noise[:, :HALF], 0.0), 0)
    inverse_11 = t_ref[:, pl.ds(HALF, HALF)]
    inverse_ref[pl.ds(0, HALF), pl.ds(0, HALF)] = inverse_11
    inverse_ref[pl.ds(0, HALF), pl.ds(HALF, HALF)] = jnp.zeros((HALF, HALF), jnp.float32)
    factor_ref[pl.ds(0, HALF), pl.ds(0, HALF)] = t_ref[:, pl.ds(0, HALF)].T
    factor_ref[pl.ds(0, HALF), pl.ds(HALF, HALF)] = jnp.zeros((HALF, HALF), jnp.float32)
    lower = dot(blocks[1], inverse_11, ((1,), (1,)))
    factor_ref[pl.ds(HALF, HALF), pl.ds(0, HALF)] = lower
    half(
        blocks[2]
        + jnp.where(unit, head_noise[:, HALF:], 0.0)
        - dot(lower, lower, ((1,), (1,))),
        1,
    )
    inverse_22 = t_ref[:, pl.ds(HALF, HALF)]
    inverse_ref[pl.ds(HALF, HALF), pl.ds(HALF, HALF)] = inverse_22
    factor_ref[pl.ds(HALF, HALF), pl.ds(HALF, HALF)] = t_ref[:, pl.ds(0, HALF)].T
    lower = factor_ref[pl.ds(HALF, HALF), pl.ds(0, HALF)]
    inverse_ref[pl.ds(HALF, HALF), pl.ds(0, HALF)] = -dot(
        inverse_22, dot(lower, inverse_ref[pl.ds(0, HALF), pl.ds(0, HALF)])
    )
    last = 2 * steps - 1
    goal = chunk_goal(last)

    def keep_up(goal, more, wanted=True):
        more = jnp.where(has_far & wanted, more, 0)
        takes(goal, goal + more)
        return goal + more


    inverse = inverse_ref[...]
    solver[:, pl.ds(0, PB)] = stacked(inverse.T)
    solver[:, pl.ds(PB, PB)] = stacked(dot(inverse, inverse, ((0,), (0,))))

    goal = keep_up(goal, jnp.where(plane == 1, PUSH[0], PUSH[1]))
    each(row_goal(last), ROW_CHUNKS, row_forward)
    run(r == 0, head_copy.wait)
    run(~even, lambda: each(0, head_chunks, chunk_take))
    head_ref[...] = dot(inverse, col_raw[:, head_span])
    goal = keep_up(goal, 1)

    def row_wait(j):
        for way in range(2):
            run((place > 0) & ~forwards(way), row_copies(j, way, False).wait_recv)

    each(0, ROW_CHUNKS - LATE, row_wait)
    for j in range(LATE):
        goal = keep_up(goal, 1, (c > 0) & (place != half_ring))
        row_wait(ROW_CHUNKS - LATE + j)
    run(c == 0, row_copy.wait)
    need_start()
    each(min(steps, pairs), pairs, lambda p: cov_copy(p).start())

    def solve(i, carry):
        rows = pl.ds(pl.multiple_of(i * PB, PB), PB)
        high, low = split(row_raw[rows, :])
        both = jnp.dot(
            jnp.concatenate([high, low, high], axis=1),
            solver[...],
            preferred_element_type=jnp.float32,
        )
        panel[rows, :] = both[:, :PB]
        high, low = split(both[:, PB:])
        parts[rows, pl.ds(0, PB)] = high
        parts[rows, pl.ds(PB, PB)] = low
        parts[rows, pl.ds(2 * PB, PB)] = high
        return carry

    lax.fori_loop(0, row_count // PB, solve, 0)

    @pl.when(r == 0)
    def _():
        panel[pl.ds(0, PB), :] = factor_ref[...]

    goal = keep_up(goal, 1)
    target_copy.wait()
    reconstructor[...] = reconstructor[...] - jnp.dot(
        parts[...], stacked(col_raw[:, head_span]), preferred_element_type=jnp.float32
    )

    @pl.when(r == 0)
    def _():
        reconstructor[pl.ds(0, PB), :] = head_ref[...]

    goal = keep_up(goal, 1)
    run(r == 0, col_copy.wait)

    pace = jnp.where(plane == 1, PACE[0], PACE[1])

    def reach(p):
        return jnp.minimum(jnp.maximum(goal + lax.div(pace * p, 9), head_chunks + 2 * p), chunks)

    def tail_reach(p):
        reached = jnp.clip(TAIL * (goal + lax.div(pace * p, 9) - chunks) // 2, 0, TAIL)
        return jnp.where(p == pairs, TAIL, reached)

    def arrive(p):
        takes(reach(p), reach(p + 1))
        run(
            ~even & (p < pairs - 1),
            lambda: each(head_chunks + 2 * p, head_chunks + 2 * p + 2, chunk_take),
        )
        run(relays, lambda: each(tail_reach(p), tail_reach(p + 1), tail_take))
        run(~even & (p == pairs - 1), lambda: each(0, TAIL, tail_take))
        cov_copy(p).wait()

    def update(p):
        arrive(p)
        columns = pl.ds(pl.multiple_of(p * PB, PB), PB)
        update_pair(
            updated,
            columns,
            updated,
            columns,
            parts,
            col_raw[:, pl.ds(pl.multiple_of(width + p * PB, CHUNK), PB)],
            noise,
            c * col_count + p * PB - r * row_count,
            r,
        )

    def finish_product():
        run(c == owner, own_need.wait)
        run(c != owner, need_copies[0].wait_recv)
        product[...] = dot(dot(inverse, need_raw[...]), head_ref[...], ((0,), (0,)))

    def chunk_finish(q):
        copies = chunk_copies(q, col_raw.at[span(q)])
        run(has_far, copies[0].wait_send)
        run(has_near, copies[1].wait_send)

    def row_finish(j):
        for way in range(2):
            run((place == 0) | forwards(way), row_copies(j, way, False).wait_send)

    tail = pairs - MEET
    here = pairs - KEEP
    settled = jnp.where(even, jnp.minimum(head_chunks + 2 * tail, chunks) - 4, 0)

    def settle():
        for k in range(n_col):
            run((c == owner) & (c != k), need_copies[k].wait_send)
        for i in range(4):
            diag_each(i, False, r >= 0, finish)
        run(even, lambda: each(0, settled, chunk_finish))
        each(0, ROW_CHUNKS, row_finish)

    each(0, min(tail, here), update)
    each(min(tail, here), tail, arrive)
    finish_product()
    settle()

    @pl.when(c == 0)
    def _():
        updated[:, pl.ds(0, PB)] = panel[...]

    each(tail, max(tail, here), update)
    each(max(tail, here), pairs, arrive)
    late_raw[...] = col_raw[:, pl.ds(width + col_count - KEEP * PB, KEEP * PB)]

    run(even, lambda: each(settled, chunks, chunk_finish))

    def tail_finish(t):
        copies = tail_copies(t, False)
        run(has_far, copies[0].wait_send)
        run(has_near, copies[1].wait_send)

    each(0, TAIL, tail_finish)


SLABS = 6


def store_kernel(
    updated,
    reconstructor,
    panel,
    product,
    parts,
    noise,
    late_raw,
    pos,
    strength,
    scale,
    tile_layer,
    updated_out,
    reconstructor_out,
    panel_out,
    error_out,
    error,
    late,
    sems,
):
    r = lax.axis_index("row")
    c = lax.axis_index("col")
    row_count, col_count = updated.shape
    slab = row_count // SLABS
    early = pl.ds(0, col_count - KEEP * PB)
    copies = [
        pltpu.make_async_copy(
            updated.at[pl.ds(i * slab, slab), early],
            updated_out.at[pl.ds(i * slab, slab), early],
            sems.at[i],
        )
        for i in range(SLABS)
    ]
    copies.append(pltpu.make_async_copy(reconstructor, reconstructor_out, sems.at[SLABS]))
    copies.append(pltpu.make_async_copy(panel, panel_out, sems.at[SLABS + 1]))
    for copy in copies:
        copy.start()

    def late_copy(k):
        columns = pl.ds(pl.multiple_of(k * PB, PB), PB)
        place = pl.ds(pl.multiple_of(col_count - (KEEP - k) * PB, PB), PB)
        return pltpu.make_async_copy(
            late.at[:, columns], updated_out.at[:, place], sems.at[SLABS + 3 + k]
        )

    def late_update(k, carry):
        columns = pl.ds(pl.multiple_of(k * PB, PB), PB)
        first = col_count - (KEEP - k) * PB
        update_pair(
            late,
            columns,
            updated,
            pl.ds(pl.multiple_of(first, PB), PB),
            parts,
            late_raw[:, columns],
            noise,
            c * col_count + first - r * row_count,
            r,
        )
        late_copy(k).start()
        return carry

    lax.fori_loop(0, KEEP, late_update, 0)
    height, width = error.shape
    target_covariance(
        error,
        product,
        pos,
        strength,
        scale,
        tile_layer,
        pl.multiple_of(r * height, TILE),
        pl.multiple_of(c * width, TILE),
    )
    last = pltpu.make_async_copy(error, error_out, sems.at[SLABS + 2])
    last.start()
    for k in range(KEEP):
        copies.append(late_copy(k))
    for copy in copies:
        copy.wait()
    last.wait()


def local(
    n_row, n_col, covariance, wfs_map, noise_var, targets, target_pos, layer_strength,
    layer_scale, tile_layer
):
    row_count, col_count = covariance.shape
    target_width = targets.shape[1]
    error_rows = target_width * n_col // n_row
    chunks = (target_width + col_count - PB) // CHUNK

    def f32(*shape):
        return jax.ShapeDtypeStruct(shape, jnp.float32)

    vmem = pl.BlockSpec(memory_space=pltpu.VMEM)
    anywhere = pl.BlockSpec(memory_space=pltpu.HBM)
    smem = pl.BlockSpec(memory_space=pltpu.SMEM)
    dma = pltpu.SemaphoreType.DMA
    results = pl.pallas_call(
        functools.partial(panel_kernel, n_row, n_col),
        out_shape=(
            f32(row_count, col_count),
            f32(row_count, target_width),
            f32(row_count, PB),
            f32(error_rows, target_width),
            jax.ShapeDtypeStruct((row_count, 3 * PB), jnp.bfloat16),
            f32(1, row_count),
            f32(PB, KEEP * PB),
        ),
        in_specs=[anywhere] * 4,
        out_specs=[vmem] * 7,
        scratch_shapes=[
            pltpu.VMEM((row_count, PB), jnp.float32),
            pltpu.VMEM((PB, target_width + col_count), jnp.float32),
            pltpu.VMEM((PB, error_rows), jnp.float32),
            pltpu.VMEM((3, HALF, HALF), jnp.float32),
            pltpu.VMEM((PB,), jnp.int32),
            pltpu.VMEM((row_count,), jnp.int32),
            pltpu.SMEM(noise_var.shape, jnp.float32),
            pltpu.VMEM((HALF, PB), jnp.float32),
            pltpu.VMEM((PB, PB), jnp.float32),
            pltpu.VMEM((PB, PB), jnp.float32),
            pltpu.VMEM((3 * PB, 2 * PB), jnp.bfloat16),
            pltpu.VMEM((PB, target_width), jnp.float32),
            dma((11,)),
            dma((col_count // PB,)),
            dma((4, 4)),
            dma((4,)),
            dma((chunks, 2)),
            dma((chunks,)),
            dma((TAIL, 2)),
            dma((TAIL,)),
            dma((ROW_CHUNKS, 2)),
            dma((ROW_CHUNKS, 2)),
            dma((n_col,)),
            dma,
        ],
        compiler_params=pltpu.CompilerParams(
            collective_id=0, has_side_effects=True, vmem_limit_bytes=14 * 1024 * 1024
        ),
        name="panel",
    )(
        covariance,
        *[pltpu.with_memory_space_constraint(x, pltpu.HBM) for x in (targets, wfs_map, noise_var)],
    )

    outs = pl.pallas_call(
        store_kernel,
        out_shape=(
            f32(row_count, col_count),
            f32(row_count, target_width),
            f32(row_count, PB),
            f32(error_rows, target_width),
        ),
        in_specs=[vmem] * 8 + [smem] * 3,
        out_specs=[anywhere] * 4,
        scratch_shapes=[
            pltpu.VMEM((error_rows, target_width), jnp.float32),
            pltpu.VMEM((row_count, KEEP * PB), jnp.float32),
            dma((SLABS + 3 + KEEP,)),
        ],
        compiler_params=pltpu.CompilerParams(vmem_limit_bytes=8 * 1024 * 1024),
        name="store",
    )(*results, target_pos, layer_strength, layer_scale, tile_layer)
    updated, reconstructor, panel, error_cov = outs
    return updated, panel, reconstructor, error_cov


def solution(mesh):
    placed = (P("row", "col"), P("row"), P(), P("row", "col"), P(), P(), P(), P())
    return jax.shard_map(
        functools.partial(local, mesh.shape["row"], mesh.shape["col"]),
        mesh=mesh,
        in_specs=placed,
        out_specs=(P("row", "col"), P("row", None), P("row", "col"), P("row", "col")),
        check_vma=False,
    )
```
